256 devices in a mesh: gx: 32 (over y, z_hi, x), vert: 8 (over z_lo, core).
Axes of the slice: x: 4, y: 4, z: 8 (z_hi: 2, z_lo: 4; z = z_hi * 4 + z_lo), core: 2. Of those that a mesh axis runs over, the one named last changes fastest.
Arguments:
- phase_field: float32 [128, 128, 32, 256], P('vert', 'gx'), may hold values from -0.2 to 1.2
- kappa_table: float32 [24, 3], replicated, may hold values from 0.2 to 2
- eps_table: float32 [12, 6], replicated, may hold values from -0.3 to 0.3
- orient_index: int32 [128], P('vert'), may hold values from 0 to 23
- family_index: int32 [128], P('vert'), may hold values from 0 to 11
Outputs:
- phase_next: float32 [128, 128, 32, 256], P('vert', 'gx')
- stress: float32 [6, 128, 32, 256], P(None, 'gx')
The draws below stay inside these ranges and needn't reach their ends.
All inputs are finite; a program needn't handle non-finite values.
Results may differ from the reference program's by a relative error of at most 0.0003.
Values sent between devices are 32-bit elements; how exact they have to be, the bound alone decides.
No kernel may reach another device: no remote copies, remote signals or barrier semaphores. Data moves between devices by JAX's collectives and lax.ppermute only.
A program may use at most 64 MiB of HBM per device.

```python
import math
import jax
import jax.numpy as jnp
from jax import lax

NVAR = 128
NFAM = 12
NORI = 24
NY = 32
NZ = 256
NX = 128


def with_ends(values, key, low, top_value):
    dims = values.shape
    spot = [jax.random.randint(jax.random.fold_in(key, axis), (), 0, dims[axis]) for axis in range(len(dims))]
    values = values.at[tuple(spot)].set(low)
    longest = dims.index(max(dims))
    spot[longest] = (spot[longest] + 1) % dims[longest]
    return values.at[tuple(spot)].set(top_value)


def shard_levels(own_key, extent, pieces, smallest, largest):
    def one(position, blocks):
        steps = jax.random.uniform(jax.random.fold_in(jax.random.fold_in(own_key, 6), position), (blocks,), jnp.float32, smallest / len(pieces), largest / len(pieces))
        return jnp.repeat(jnp.exp(steps), extent[position] // blocks).reshape((-1,) + (1,) * (len(extent) - position - 1))

    gain = one(*pieces[0])
    for cut in pieces[1:]:
        gain = gain * one(*cut)
    return gain


def noise(key, dims, deviation, bound, kind=jnp.bfloat16):
    drawn = deviation * jax.random.normal(key, dims, jnp.float32)
    return jnp.clip(drawn, min=-bound, max=bound).astype(kind)


def setup_inputs(seed: int = 0) -> dict:
    seeds = jax.random.split(jax.random.key(seed), 6)
    phase_field = jnp.clip(-0.2 + 1.4000001 * jax.random.uniform(seeds[0], (NVAR, NX, NY, NZ), jnp.float32) ** shard_levels(seeds[0], (NVAR, NX, NY, NZ), ((0, 8), (1, 32)), -0.2, 0.2), -0.2, 1.2)
    kappa_table = jnp.clip(jnp.exp(jax.random.uniform(seeds[1], (NORI, 3), jnp.float32, math.log(0.2), math.log(2.0))), 0.2, 2.0)
    eps_table = noise(seeds[2], (NFAM, 6), 0.05, 0.3, jnp.float32)
    orient_index = with_ends(jax.random.randint(seeds[3], (NVAR,), 0, NORI), jax.random.fold_in(seeds[3], 1), 0, NORI - 1).astype(jnp.int32)
    family_index = with_ends(jax.random.randint(seeds[4], (NVAR,), 0, NFAM), jax.random.fold_in(seeds[4], 1), 0, NFAM - 1).astype(jnp.int32)
    return dict(phase_field=phase_field, kappa_table=kappa_table, eps_table=eps_table, orient_index=orient_index, family_index=family_index)


LAME_LAMBDA = 1.5
SHEAR_MOD = 1.0
TIME_STEP = 0.1
CROSS_COUPLING = 0.02
HIGHEST = lax.Precision.HIGHEST
TENSOR_SLOTS = ((0, 5, 4), (5, 1, 3), (4, 3, 2))
VOIGT_PAIRS = ((0, 0), (1, 1), (2, 2), (1, 2), (0, 2), (0, 1))

def signed_wave(first_row, row_count, full_count):
    positions = first_row + jnp.arange(row_count, dtype=jnp.int32)
    shifted = jnp.where(positions * 2 >= full_count, positions - full_count, positions)
    return shifted.astype(jnp.float32) / full_count

def wave_normals(x_wave, y_wave, z_wave):
    x_grid = x_wave[:, None, None]
    y_grid = y_wave[None, :, None]
    z_grid = z_wave[None, None, :]
    length_sq = x_grid * x_grid + y_grid * y_grid + z_grid * z_grid
    positive = length_sq > 0
    safe_length = jnp.where(positive, length_sq, 1.0)
    inverse_len = jnp.where(positive, lax.rsqrt(safe_length), 0.0)
    return [x_grid * inverse_len, y_grid * inverse_len, z_grid * inverse_len]

def green_stress(strain, normals):
    trace_strain = strain[0] + strain[1] + strain[2]
    stiffened = [LAME_LAMBDA * trace_strain + 2.0 * SHEAR_MOD * strain[number] if number < 3 else 2.0 * SHEAR_MOD * strain[number] for number in range(6)]
    traction = [sum((stiffened[TENSOR_SLOTS[row_axis][col_axis]] * normals[col_axis] for col_axis in range(3))) for row_axis in range(3)]
    normal_part = normals[0] * traction[0] + normals[1] * traction[1] + normals[2] * traction[2]
    coupling = (LAME_LAMBDA + SHEAR_MOD) / (LAME_LAMBDA + 2.0 * SHEAR_MOD)
    shifted = [(traction[row_axis] - normals[row_axis] * normal_part * coupling) / SHEAR_MOD for row_axis in range(3)]
    excess = [0.5 * (normals[VOIGT_PAIRS[number][0]] * shifted[VOIGT_PAIRS[number][1]] + normals[VOIGT_PAIRS[number][1]] * shifted[VOIGT_PAIRS[number][0]]) - strain[number] for number in range(6)]
    trace_excess = excess[0] + excess[1] + excess[2]
    result = [LAME_LAMBDA * trace_excess + 2.0 * SHEAR_MOD * excess[number] if number < 3 else 2.0 * SHEAR_MOD * excess[number] for number in range(6)]
    return jnp.stack(result)

def reaction_update(variant, laplace, driving, square_sum):
    chemical = 2.0 * variant - 6.0 * variant * variant + 4.0 * variant * variant * variant
    chemical = chemical + 2.0 * CROSS_COUPLING * variant * (square_sum - variant * variant)
    chemical = chemical - 2.0 * variant * driving - laplace
    return variant - TIME_STEP * chemical

def reference(phase_field, kappa_table, eps_table, orient_index, family_index):
    family_hot = (family_index[:, None] == jnp.arange(NFAM, dtype=jnp.int32)[None, :]).astype(jnp.float32)
    orient_hot = (orient_index[:, None] == jnp.arange(NORI, dtype=jnp.int32)[None, :]).astype(jnp.float32)
    eps_var = jnp.dot(family_hot, eps_table, precision=HIGHEST)
    kappa_var = jnp.dot(orient_hot, kappa_table, precision=HIGHEST)

    def accumulate(state_pair, inputs):
        eigen_sum, square_sum = state_pair
        variant, strain_row = inputs
        squared = variant * variant
        return ((eigen_sum + strain_row[:, None, None, None] * squared[None], square_sum + squared), None)
    start_eigen = jnp.zeros((6, NX, NY, NZ), jnp.float32)
    start_square = jnp.zeros((NX, NY, NZ), jnp.float32)
    (eigen_sum, square_sum), unused = lax.scan(accumulate, (start_eigen, start_square), (phase_field, eps_var))
    eigen_hat = jnp.fft.fftn(eigen_sum, axes=(1, 2, 3))
    normals = wave_normals(signed_wave(0, NX, NX), signed_wave(0, NY, NY), signed_wave(0, NZ, NZ))
    real_hat = green_stress(jnp.real(eigen_hat).astype(jnp.float32), normals)
    imag_hat = green_stress(jnp.imag(eigen_hat).astype(jnp.float32), normals)
    stress = jnp.real(jnp.fft.ifftn(real_hat + 1j * imag_hat, axes=(1, 2, 3))).astype(jnp.float32)
    weights = jnp.array([1.0, 1.0, 1.0, 2.0, 2.0, 2.0], jnp.float32)

    def advance(inputs):
        variant, strain_row, kappa_row = inputs
        driving = jnp.einsum('k,kxyz->xyz', strain_row * weights, stress, precision=HIGHEST)
        laplace = kappa_row[0] * (jnp.roll(variant, 1, 0) + jnp.roll(variant, -1, 0) - 2.0 * variant)
        laplace = laplace + kappa_row[1] * (jnp.roll(variant, 1, 1) + jnp.roll(variant, -1, 1) - 2.0 * variant)
        laplace = laplace + kappa_row[2] * (jnp.roll(variant, 1, 2) + jnp.roll(variant, -1, 2) - 2.0 * variant)
        return reaction_update(variant, laplace, driving, square_sum)
    phase_next = lax.map(advance, (phase_field, eps_var, kappa_var))
    return (phase_next, stress)
```

```python
import functools

import jax
import jax.numpy as jnp
import numpy as np
from jax import lax
from jax.experimental import pallas as pl
from jax.experimental.pallas import tpu as pltpu
from jax.sharding import PartitionSpec as P

LAME_LAMBDA = 1.5
SHEAR_MOD = 1.0
TIME_STEP = 0.1
CROSS_COUPLING = 0.02
TENSOR_SLOTS = ((0, 5, 4), (5, 1, 3), (4, 3, 2))
VOIGT_PAIRS = ((0, 0), (1, 1), (2, 2), (1, 2), (0, 2), (0, 1))
F32 = jnp.float32
BF16 = jnp.bfloat16
NX, NY, NZ = 128, 32, 256
SLAB = 4
SLABS = 32
HALF = NZ // 2
COMPS = 6


def z_table():
    z = np.arange(NZ)
    kz = np.arange(HALF)
    angle = 2 * np.pi * (np.outer(kz, z) % NZ) / NZ
    imag = -np.sin(angle)
    imag[0] = (-1.0) ** z
    return np.concatenate([np.cos(angle), imag])


def y_tables():
    general = np.zeros((2, SLAB, NY, 2, 2, SLAB, 16))
    packed = np.zeros((2, SLAB, NY, 2, 2, SLAB, 16))
    y = np.arange(NY)
    for half in range(2):
        for low in range(16):
            angle = 2 * np.pi * ((16 * half + low) * y % NY) / NY
            plain = 2 * np.pi * (low * y % NY) / NY
            for x in range(SLAB):
                general[0, x, :, half, 0, x, low] = np.cos(angle)
                general[1, x, :, half, 0, x, low] = np.sin(angle)
                general[0, x, :, half, 1, x, low] = -np.sin(angle)
                general[1, x, :, half, 1, x, low] = np.cos(angle)
                packed[half, x, :, half, 0, x, low] = np.cos(plain)
                packed[half, x, :, half, 1, x, low] = -np.sin(plain) if low else (-1.0) ** y
    return general.reshape(256, 256), packed.reshape(256, 256)


def x_tables():
    slab = np.arange(SLABS)
    angle = 2 * np.pi * (np.outer(slab, slab) % SLABS) / SLABS
    cosine, sine = np.cos(angle), np.sin(angle)
    left = np.zeros((COMPS, SLABS, 2, SLABS, 8))
    back = np.zeros((SLABS, 8, 2, COMPS, SLABS))
    for comp in range(COMPS):
        left[comp, :, 0, :, comp] = cosine
        left[comp, :, 1, :, comp] = sine
        back[:, comp, 0, comp, :] = cosine / NX
        back[:, comp, 1, comp, :] = -sine / NX
    lane = np.arange(128)
    plane = lane // 16 % SLAB
    turn = 2 * np.pi * np.outer(slab, plane) / NX
    right = np.zeros((2, SLAB, 16, 2, SLAB, 16))
    for plane_in in range(SLAB):
        for plane_out in range(SLAB):
            theta = 2 * np.pi * (plane_in * plane_out % SLAB) / SLAB
            for low in range(16):
                right[0, plane_in, low, 0, plane_out, low] = np.round(np.cos(theta))
                right[1, plane_in, low, 0, plane_out, low] = np.round(np.sin(theta))
                right[0, plane_in, low, 1, plane_out, low] = -np.round(np.sin(theta))
                right[1, plane_in, low, 1, plane_out, low] = np.round(np.cos(theta))
    right = right.reshape(128, 128)
    return left.reshape(192, 512), back.reshape(256, 384), np.cos(turn), np.sin(turn), right, right.T.copy()


def halves_of(table):
    full = np.asarray(table, np.float32)
    high = full.astype(jnp.bfloat16)
    low = (table - high.astype(np.float64)).astype(jnp.bfloat16)
    return jnp.asarray(high), jnp.asarray(low)


PLAIN = (((1,), (0,)), ((), ()))
RIGHT_T = (((1,), (1,)), ((), ()))
LEFT_T = (((0,), (0,)), ((), ()))


def split(value):
    high = value.astype(BF16)
    return high, (value - high.astype(F32)).astype(BF16)


def mul(a, b, dims):
    return lax.dot_general(a, b, dims, preferred_element_type=F32)


def dot3(left, right, dims=PLAIN):
    return mul(left[0], right[0], dims) + (mul(left[0], right[1], dims) + mul(left[1], right[0], dims))


def sums_kernel(core_ref, family_ref, eps_ref, phase_ref, tzh, tzl, ryh, ryl, rph, rpl, keep_ref, send_ref, eigen, square):
    step = pl.program_id(0)
    variants = phase_ref.shape[0]
    weight = [[eps_ref[family_ref[v], k] for k in range(COMPS)] for v in range(variants)]
    for tile in range(NY // 8):
        total = [None] * COMPS
        plain = None
        for v in range(variants):
            value = phase_ref[v, 0, tile * 8 : tile * 8 + 8, :]
            value = value * value
            plain = value if plain is None else plain + value
            for k in range(COMPS):
                term = weight[v][k] * value
                total[k] = term if total[k] is None else total[k] + term
        row = pl.multiple_of(step * NY + tile * 8, 8)
        square[pl.ds(row, 8), :] = plain
        for k in range(COMPS):
            eigen[pl.ds(k * 128 + row, 8), :] = total[k]

    @pl.when(step == SLAB - 1)
    def _():
        first = core_ref[0] == 0
        along_z = dot3((tzh[...], tzl[...]), split(eigen[...]), RIGHT_T)
        lines = []
        for k in range(COMPS):
            block = along_z[:, k * 128 : k * 128 + 128]
            lines.append(jnp.concatenate([block[:HALF], block[HALF:]], axis=1))
        packed_rows = jnp.concatenate([line[:8] for line in lines], axis=0)
        along_y = dot3(split(jnp.concatenate(lines, axis=0)), (ryh[...], ryl[...]))
        packed = dot3(split(packed_rows), (rph[...], rpl[...]))
        top = lax.broadcasted_iota(jnp.int32, (8, 256), 0) == 0
        for k in range(COMPS):
            block = along_y[k * 128 : k * 128 + 128]
            head = jnp.where(top, packed[k * 8 : k * 8 + 8], block[:8])
            block = jnp.concatenate([head, block[8:]], axis=0)
            keep_ref[pl.ds(k, 128, stride=8), :] = jnp.where(first, block[:, :128], block[:, 128:])
            send_ref[pl.ds(k, 128, stride=8), :] = jnp.where(first, block[:, 128:], block[:, :128])
        sums = square[...]
        keep_ref[pl.ds(6, 128, stride=8), :] = jnp.where(first, sums[:, :128], sums[:, 128:])
        send_ref[pl.ds(6, 128, stride=8), :] = jnp.where(first, sums[:, 128:], sums[:, :128])
        empty = jnp.zeros((128, 128), F32)
        keep_ref[pl.ds(7, 128, stride=8), :] = empty
        send_ref[pl.ds(7, 128, stride=8), :] = empty


def green_stress(strain, normals):
    trace_strain = strain[0] + strain[1] + strain[2]
    stiffened = [
        LAME_LAMBDA * trace_strain + 2.0 * SHEAR_MOD * strain[number] if number < 3 else 2.0 * SHEAR_MOD * strain[number]
        for number in range(6)
    ]
    traction = [sum(stiffened[TENSOR_SLOTS[row][col]] * normals[col] for col in range(3)) for row in range(3)]
    normal_part = normals[0] * traction[0] + normals[1] * traction[1] + normals[2] * traction[2]
    coupling = (LAME_LAMBDA + SHEAR_MOD) / (LAME_LAMBDA + 2.0 * SHEAR_MOD)
    shifted = [(traction[row] - normals[row] * normal_part * coupling) * (1.0 / SHEAR_MOD) for row in range(3)]
    excess = [
        0.5 * (normals[a] * shifted[b] + normals[b] * shifted[a]) - strain[number]
        for number, (a, b) in enumerate(VOIGT_PAIRS)
    ]
    trace_excess = excess[0] + excess[1] + excess[2]
    return [
        LAME_LAMBDA * trace_excess + 2.0 * SHEAR_MOD * excess[number] if number < 3 else 2.0 * SHEAR_MOD * excess[number]
        for number in range(6)
    ]


def unit(wave):
    length_sq = wave[0] * wave[0] + wave[1] * wave[1] + wave[2] * wave[2]
    positive = length_sq > 0
    inverse = jnp.where(positive, lax.rsqrt(jnp.where(positive, length_sq, 1.0)), 0.0)
    return [part * inverse for part in wave]


def spectral_kernel(place_ref, in_ref, lh, ll, bh, bl, tc_ref, ts_ref, right_ref, inverse_ref, out_ref):
    half, kz = place_ref[0], place_ref[1]
    rows = ((in_ref[:, 0] + in_ref[:, 1]) + (in_ref[:, 2] + in_ref[:, 3])).reshape(256, 128)
    lane1 = lax.broadcasted_iota(jnp.int32, (1, 128), 1)
    sign = jnp.where(lane1 < 64, 1.0, -1.0).astype(F32)

    def turned(value):
        return pltpu.roll(value, 64, 1) * sign

    flipped = rows * sign
    stacked = jnp.concatenate(
        [
            jnp.concatenate([rows, flipped], axis=1),
            jnp.concatenate([turned(rows), turned(flipped)], axis=1),
        ],
        axis=0,
    )
    spread = dot3((lh[...], ll[...]), split(stacked))
    both = jnp.concatenate([spread[:, :128], spread[:, 128:]], axis=0)
    cosine = tc_ref[...][None]
    sine = ts_ref[...][None]
    both = (both.reshape(12, 32, 128) * cosine + turned(both).reshape(12, 32, 128) * sine).reshape(384, 128)
    high, low = split(both)
    right = right_ref[...]
    hat = (mul(high, right, PLAIN) + mul(low, right, PLAIN)).reshape(12, 32, 128)

    row = lax.broadcasted_iota(jnp.int32, (32, 128), 0)
    lane = lax.broadcasted_iota(jnp.int32, (32, 128), 1)
    low_y = lane % 16
    kx = row + 32 * (lane // 16 % SLAB)
    plane = kz == 0
    ky = jnp.where(plane, low_y, 16 * half + low_y)
    wave_x = jnp.where(kx >= NX // 2, kx - NX, kx).astype(F32) * (1.0 / NX)
    wave_y = jnp.where(ky >= NY // 2, ky - NY, ky).astype(F32) * (1.0 / NY)
    kz_own = jnp.where(plane, jnp.where(half == 1, -HALF, 0), kz)
    wave_z = jnp.full((32, 128), kz_own, jnp.int32).astype(F32) * (1.0 / NZ)
    flip_x = jnp.where(kx == NX // 2, -wave_x, wave_x)
    flip_y = jnp.where(ky == NY // 2, -wave_y, wave_y)
    flip_z = jnp.where(jnp.full((32, 128), kz_own, jnp.int32) == -HALF, -wave_z, wave_z)
    special = jnp.logical_and(jnp.full((32, 128), kz, jnp.int32) == 0, low_y == 0)
    edge_y = jnp.full((32, 128), -0.5, F32)

    first, second = [], []
    for k in range(COMPS):
        a, b = hat[k], hat[k + COMPS]
        first.append(jnp.where(special, 0.5 * (a + b), a))
        second.append(jnp.where(special, 0.5 * (a - b), 0.0))
    parts = [
        green_stress(first, unit([wave_x, wave_y, wave_z])),
        green_stress(first, unit([flip_x, flip_y, flip_z])),
        green_stress(second, unit([wave_x, edge_y, wave_z])),
        green_stress(second, unit([flip_x, -edge_y, flip_z])),
    ]
    result = [0.5 * ((parts[0][k] + parts[1][k]) + (parts[2][k] + parts[3][k])) for k in range(COMPS)]

    high, low = split(jnp.concatenate(result, axis=0))
    inverse = inverse_ref[...]
    value = mul(high, inverse, PLAIN) + mul(low, inverse, PLAIN)
    value = (value.reshape(6, 32, 128) * cosine - turned(value).reshape(6, 32, 128) * sine).reshape(192, 128)
    stacked = jnp.concatenate([value, turned(value)], axis=0)
    answer = dot3((bh[...], bl[...]), split(stacked))
    kind = lax.broadcasted_iota(jnp.int32, (256, 128), 0) % 8
    answer = jnp.where(kind == 6, rows, answer).reshape(32, 8, 128)
    for copy in range(out_ref.shape[1]):
        out_ref[:, copy] = answer


def update_kernel(
    core_ref, family_ref, orient_ref, eps_ref, kappa_ref, mine_ref, other_ref, phase_ref, low_ref, high_ref,
    ryh, ryl, rph, rpl, tzh, tzl, next_ref, stress_ref, base,
):
    step = pl.program_id(0)

    @pl.when(step == 0)
    def _():
        first = core_ref[0] == 0

        def line(k):
            mine = mine_ref[pl.ds(k, 128, stride=8), :]
            other = other_ref[pl.ds(k, 128, stride=8), :]
            return jnp.concatenate([jnp.where(first, mine, other), jnp.where(first, other, mine)], axis=1)

        lines = [line(k) for k in range(COMPS)]
        packed = dot3(split(jnp.concatenate([block[:8] for block in lines], axis=0)), (rph[...], rpl[...]))
        along_y = dot3(split(jnp.concatenate(lines, axis=0)), (ryh[...], ryl[...]))
        top = lax.broadcasted_iota(jnp.int32, (8, 256), 0) == 0
        for k in range(COMPS):
            block = along_y[k * 128 : k * 128 + 128]
            head = jnp.where(top, packed[k * 8 : k * 8 + 8], block[:8])
            block = jnp.concatenate([head, block[8:]], axis=0)
            block = jnp.concatenate([block[:, :128], block[:, 128:]], axis=0)
            cells = dot3(split(block.T), (tzh[...], tzl[...]))
            stress_ref[k] = cells.reshape(SLAB, NY, NZ)
        base[...] = (2.0 + 2.0 * CROSS_COUPLING * line(6)).reshape(SLAB, NY, NZ)

    per_step = phase_ref.shape[0]
    for index in range(per_step):
        variant = step * per_step + index
        family = family_ref[variant]
        orient = orient_ref[variant]
        weight = [eps_ref[family, k] * (-2.0 if k < 3 else -4.0) for k in range(COMPS)]
        kappa = [TIME_STEP * kappa_ref[orient, d] for d in range(3)]
        center = 1.0 - 2.0 * (0.0 + kappa[0] + kappa[1] + kappa[2])
        for x in range(SLAB):
            p = phase_ref[index, x]
            before = low_ref[index, 0] if x == 0 else phase_ref[index, x - 1]
            after = high_ref[index, 0] if x == SLAB - 1 else phase_ref[index, x + 1]
            slope = base[x]
            for k in range(COMPS):
                slope = slope + weight[k] * stress_ref[k, x]
            slope = slope + p * (-6.0 + (4.0 - 2.0 * CROSS_COUPLING) * p)
            moved = kappa[0] * (before + after)
            moved = moved + kappa[1] * (pltpu.roll(p, 1, 0) + pltpu.roll(p, NY - 1, 0))
            moved = moved + kappa[2] * (pltpu.roll(p, 1, 1) + pltpu.roll(p, NZ - 1, 1))
            next_ref[index, x] = p * (center - TIME_STEP * slope) + moved


def vmem():
    return pl.BlockSpec(memory_space=pltpu.VMEM)


def smem():
    return pl.BlockSpec(memory_space=pltpu.SMEM)


def ring(count, shift):
    return [(i, (i + shift) % count) for i in range(count)]


def body(phase_field, kappa_table, eps_table, orient_index, family_index):
    slabs = lax.axis_size("gx")
    groups = lax.axis_size("vert")
    runs = groups // 2
    variants = phase_field.shape[0]
    place = lax.axis_index("vert")
    core = (place % 2).astype(jnp.int32)
    kz_own = (lax.axis_index("gx") * runs + place // 2).astype(jnp.int32)
    core_arr = core.reshape(1)
    place_arr = jnp.stack([core, kz_own])

    low_plane = lax.ppermute(lax.slice_in_dim(phase_field, SLAB - 1, SLAB, axis=1), "gx", ring(slabs, 1))
    high_plane = lax.ppermute(lax.slice_in_dim(phase_field, 0, 1, axis=1), "gx", ring(slabs, -1))

    tz = z_table()
    ry, rp = y_tables()
    left, back, tc, ts, right, right_t = x_tables()

    spread = jax.ShapeDtypeStruct((1024, 128), F32)
    keep, send = pl.pallas_call(
        sums_kernel,
        grid=(SLAB,),
        in_specs=[smem(), smem(), smem(), pl.BlockSpec((variants, 1, NY, NZ), lambda i: (0, i, 0, 0))] + [vmem()] * 6,
        out_specs=[pl.BlockSpec((1024, 128), lambda i: (0, 0))] * 2,
        out_shape=[spread, spread],
        scratch_shapes=[pltpu.VMEM((COMPS * 128, NZ), F32), pltpu.VMEM((128, NZ), F32)],
        name="sums",
    )(core_arr, family_index, eps_table, phase_field, *halves_of(tz), *halves_of(ry), *halves_of(rp))

    partner = [(i, i ^ 1) for i in range(groups)]
    same_core = [[g * groups + 2 * r + c for g in range(slabs) for r in range(runs)] for c in range(2)]

    def exchange(value):
        return lax.all_to_all(
            value, ("gx", "vert"), split_axis=0, concat_axis=0, axis_index_groups=same_core, tiled=True
        )

    summed = keep + lax.ppermute(send, "vert", partner)
    arrived = exchange(summed.reshape(128, 8, 128)).reshape(slabs, runs, 8, 128)

    answers = pl.pallas_call(
        spectral_kernel,
        in_specs=[smem()] + [vmem()] * 9,
        out_specs=vmem(),
        out_shape=jax.ShapeDtypeStruct((slabs, runs, 8, 128), F32),
        name="spectral",
    )(
        place_arr, arrived, *halves_of(left), *halves_of(back), jnp.asarray(tc, F32), jnp.asarray(ts, F32),
        jnp.asarray(right, BF16), jnp.asarray(right_t, BF16),
    )

    mine = exchange(answers.reshape(128, 8, 128)).reshape(1024, 128)
    other = lax.ppermute(mine, "vert", partner)

    per_step = 2
    phase_next, stress = pl.pallas_call(
        update_kernel,
        grid=(variants // per_step,),
        in_specs=[smem()] * 5
        + [vmem()] * 2
        + [
            pl.BlockSpec((per_step, SLAB, NY, NZ), lambda i: (i, 0, 0, 0)),
            pl.BlockSpec((per_step, 1, NY, NZ), lambda i: (i, 0, 0, 0)),
            pl.BlockSpec((per_step, 1, NY, NZ), lambda i: (i, 0, 0, 0)),
        ]
        + [vmem()] * 6,
        out_specs=[
            pl.BlockSpec((per_step, SLAB, NY, NZ), lambda i: (i, 0, 0, 0)),
            pl.BlockSpec((COMPS, SLAB, NY, NZ), lambda i: (0, 0, 0, 0)),
        ],
        out_shape=[
            jax.ShapeDtypeStruct(phase_field.shape, F32),
            jax.ShapeDtypeStruct((COMPS, SLAB, NY, NZ), F32),
        ],
        scratch_shapes=[pltpu.VMEM((SLAB, NY, NZ), F32)],
        name="update",
    )(
        core_arr, family_index, orient_index, eps_table, kappa_table, mine, other, phase_field, low_plane, high_plane,
        *halves_of(np.linalg.inv(ry)), *halves_of(np.linalg.inv(rp)), *halves_of(np.linalg.inv(tz).T),
    )
    return phase_next, stress


def solution(mesh):
    return jax.shard_map(
        body,
        mesh=mesh,
        in_specs=(P("vert", "gx", None, None), P(), P(), P("vert"), P("vert")),
        out_specs=(P("vert", "gx", None, None), P(None, "gx", None, None)),
        check_vma=False,
    )
```

```python
import jax
import jax.numpy as jnp
import numpy as np
from jax import lax
from jax.experimental import pallas as pl
from jax.experimental.pallas import tpu as pltpu
from jax.sharding import PartitionSpec as P


LAME_LAMBDA = 1.5
SHEAR_MOD = 1.0
TIME_STEP = 0.1
CROSS_COUPLING = 0.02
TENSOR_SLOTS = ((0, 5, 4), (5, 1, 3), (4, 3, 2))
VOIGT_PAIRS = ((0, 0), (1, 1), (2, 2), (1, 2), (0, 2), (0, 1))
F32 = jnp.float32
BF16 = jnp.bfloat16
NX, NY, NZ = 128, 32, 256
SLAB = 4
SLABS = 32
HALF = NZ // 2
COMPS = 6


def z_table():
    z = np.arange(NZ)
    kz = np.arange(HALF)
    angle = 2 * np.pi * (np.outer(kz, z) % NZ) / NZ
    imag = -np.sin(angle)
    imag[0] = (-1.0) ** z
    return np.concatenate([np.cos(angle), imag])


def y_tables():
    general = np.zeros((2, SLAB, NY, 2, 2, SLAB, 16))
    packed = np.zeros((2, SLAB, NY, 2, 2, SLAB, 16))
    y = np.arange(NY)
    for half in range(2):
        for low in range(16):
            angle = 2 * np.pi * ((16 * half + low) * y % NY) / NY
            plain = 2 * np.pi * (low * y % NY) / NY
            for x in range(SLAB):
                general[0, x, :, half, 0, x, low] = np.cos(angle)
                general[1, x, :, half, 0, x, low] = np.sin(angle)
                general[0, x, :, half, 1, x, low] = -np.sin(angle)
                general[1, x, :, half, 1, x, low] = np.cos(angle)
                packed[half, x, :, half, 0, x, low] = np.cos(plain)
                packed[half, x, :, half, 1, x, low] = -np.sin(plain) if low else (-1.0) ** y
    return general.reshape(256, 256), packed.reshape(256, 256)


def x_tables():
    slab = np.arange(SLABS)
    angle = 2 * np.pi * (np.outer(slab, slab) % SLABS) / SLABS
    cosine, sine = np.cos(angle), np.sin(angle)
    left = np.zeros((COMPS, SLABS, 2, SLABS, 8))
    back = np.zeros((SLABS, 8, 2, COMPS, SLABS))
    for comp in range(COMPS):
        left[comp, :, 0, :, comp] = cosine
        left[comp, :, 1, :, comp] = sine
        back[:, comp, 0, comp, :] = cosine / NX
        back[:, comp, 1, comp, :] = -sine / NX
    lane = np.arange(128)
    plane = lane // 16 % SLAB
    turn = 2 * np.pi * np.outer(slab, plane) / NX
    right = np.zeros((2, SLAB, 16, 2, SLAB, 16))
    for plane_in in range(SLAB):
        for plane_out in range(SLAB):
            theta = 2 * np.pi * (plane_in * plane_out % SLAB) / SLAB
            for low in range(16):
                right[0, plane_in, low, 0, plane_out, low] = np.round(np.cos(theta))
                right[1, plane_in, low, 0, plane_out, low] = np.round(np.sin(theta))
                right[0, plane_in, low, 1, plane_out, low] = -np.round(np.sin(theta))
                right[1, plane_in, low, 1, plane_out, low] = np.round(np.cos(theta))
    right = right.reshape(128, 128)
    return left.reshape(192, 512), back.reshape(256, 384), np.cos(turn), np.sin(turn), right, right.T.copy()


def halves_of(table):
    full = np.asarray(table, np.float32)
    high = full.astype(jnp.bfloat16)
    low = (table - high.astype(np.float64)).astype(jnp.bfloat16)
    return high, low


def stacked_halves(*tables):
    parts = [half for table in tables for half in halves_of(table)]
    return jnp.asarray(np.stack(parts))


def spectral_tables(left, back, tc, ts, right, right_t):
    packed = np.zeros((896, 512), jnp.bfloat16)
    left_high, left_low = halves_of(left)
    back_high, back_low = halves_of(back)
    packed[0:192], packed[192:384] = left_high, left_low
    packed[384:640, :384], packed[640:896, :384] = back_high, back_low
    packed[384:512, 384:], packed[512:640, 384:] = right, right_t
    for index, part in enumerate(halves_of(tc) + halves_of(ts)):
        packed[640 + 32 * index : 672 + 32 * index, 384:] = part
    return jnp.asarray(packed)


PLAIN = (((1,), (0,)), ((), ()))
RIGHT_T = (((1,), (1,)), ((), ()))


def split(value):
    high = value.astype(BF16)
    return high, (value - high.astype(F32)).astype(BF16)


def mul(a, b, dims):
    return lax.dot_general(a, b, dims, preferred_element_type=F32)


def dot3(left, right, dims=PLAIN):
    return mul(left[0], right[0], dims) + (mul(left[0], right[1], dims) + mul(left[1], right[0], dims))


def sums_kernel(
    place_ref, family_ref, eps_ref, phase_hbm, table_hbm,
    keep_ref, send_ref, last_a, last_b, front_a, front_b, phase, table, eigen, square, sems,
):
    variants = phase.shape[0]
    loads = [pltpu.make_async_copy(phase_hbm.at[:, x], phase.at[:, x], sems.at[x]) for x in range(SLAB)]
    loads.append(pltpu.make_async_copy(table_hbm, table, sems.at[SLAB]))
    for load in loads:
        load.start()
    weight = [[eps_ref[k, family_ref[v]] for k in range(COMPS)] for v in range(variants)]
    for x in range(SLAB):
        loads[x].wait()

        def tile_sum(tile, carry, x=x):
            row = pl.multiple_of(tile * 8, 8)
            total = [None] * COMPS
            plain = None
            for v in range(variants):
                value = phase[v, x, pl.ds(row, 8), :]
                value = value * value
                plain = value if plain is None else plain + value
                for k in range(COMPS):
                    term = weight[v][k] * value
                    total[k] = term if total[k] is None else total[k] + term
            square[pl.ds(x * NY + row, 8), :] = plain
            for k in range(COMPS):
                eigen[pl.ds(k * 128 + x * NY + row, 8), :] = total[k]
            return carry

        lax.fori_loop(0, NY // 8, tile_sum, 0)
        if x in (0, SLAB - 1):
            low_half, high_half = (front_a, front_b) if x == 0 else (last_a, last_b)
            low_half[...] = phase[: variants // 2, x]
            high_half[...] = phase[variants // 2 :, x]
    loads[SLAB].wait()

    first = place_ref[0] == 0
    along_z = dot3((table[0], table[1]), split(eigen[...]), RIGHT_T)
    lines = []
    for k in range(COMPS):
        block = along_z[:, k * 128 : k * 128 + 128]
        lines.append(jnp.concatenate([block[:HALF], block[HALF:]], axis=1))
    packed_rows = jnp.concatenate([line[:8] for line in lines], axis=0)
    along_y = dot3(split(jnp.concatenate(lines, axis=0)), (table[2], table[3]))
    packed = dot3(split(packed_rows), (table[4], table[5]))
    top = lax.broadcasted_iota(jnp.int32, (8, 256), 0) == 0
    for k in range(COMPS):
        block = along_y[k * 128 : k * 128 + 128]
        head = jnp.where(top, packed[k * 8 : k * 8 + 8], block[:8])
        block = jnp.concatenate([head, block[8:]], axis=0)
        keep_ref[pl.ds(k, 128, stride=8), :] = jnp.where(first, block[:, :128], block[:, 128:])
        send_ref[pl.ds(k, 128, stride=8), :] = jnp.where(first, block[:, 128:], block[:, :128])
    sums = square[...]
    keep_ref[pl.ds(6, 128, stride=8), :] = jnp.where(first, sums[:, :128], sums[:, 128:])
    send_ref[pl.ds(6, 128, stride=8), :] = jnp.where(first, sums[:, 128:], sums[:, :128])
    empty = jnp.zeros((128, 128), F32)
    keep_ref[pl.ds(7, 128, stride=8), :] = empty
    send_ref[pl.ds(7, 128, stride=8), :] = empty


def green_stress(strain, normals):
    trace_strain = strain[0] + strain[1] + strain[2]
    stiffened = [
        LAME_LAMBDA * trace_strain + 2.0 * SHEAR_MOD * strain[number] if number < 3 else 2.0 * SHEAR_MOD * strain[number]
        for number in range(6)
    ]
    traction = [sum(stiffened[TENSOR_SLOTS[row][col]] * normals[col] for col in range(3)) for row in range(3)]
    normal_part = normals[0] * traction[0] + normals[1] * traction[1] + normals[2] * traction[2]
    coupling = (LAME_LAMBDA + SHEAR_MOD) / (LAME_LAMBDA + 2.0 * SHEAR_MOD)
    shifted = [(traction[row] - normals[row] * normal_part * coupling) * (1.0 / SHEAR_MOD) for row in range(3)]
    excess = [
        0.5 * (normals[a] * shifted[b] + normals[b] * shifted[a]) - strain[number]
        for number, (a, b) in enumerate(VOIGT_PAIRS)
    ]
    trace_excess = excess[0] + excess[1] + excess[2]
    return [
        LAME_LAMBDA * trace_excess + 2.0 * SHEAR_MOD * excess[number] if number < 3 else 2.0 * SHEAR_MOD * excess[number]
        for number in range(6)
    ]


def unit(wave):
    length_sq = wave[0] * wave[0] + wave[1] * wave[1] + wave[2] * wave[2]
    positive = length_sq > 0
    inverse = jnp.where(positive, lax.rsqrt(jnp.where(positive, length_sq, 1.0)), 0.0)
    return [part * inverse for part in wave]


def spectral_kernel(place_ref, in_ref, table, out_ref):
    half, kz = place_ref[0], place_ref[1]
    rows = ((in_ref[:, 0] + in_ref[:, 1]) + (in_ref[:, 2] + in_ref[:, 3])).reshape(256, 128)
    lane1 = lax.broadcasted_iota(jnp.int32, (1, 128), 1)
    sign = jnp.where(lane1 < 64, 1.0, -1.0).astype(F32)

    def turned(value):
        return pltpu.roll(value, 64, 1) * sign

    flipped = rows * sign
    stacked = jnp.concatenate(
        [
            jnp.concatenate([rows, flipped], axis=1),
            jnp.concatenate([turned(rows), turned(flipped)], axis=1),
        ],
        axis=0,
    )
    spread = dot3((table[0:192], table[192:384]), split(stacked))
    both = jnp.concatenate([spread[:, :128], spread[:, 128:]], axis=0)
    turns = table[640:768, 384:].astype(F32)
    cosine = (turns[0:32] + turns[32:64])[None]
    sine = (turns[64:96] + turns[96:128])[None]
    both = (both.reshape(12, 32, 128) * cosine + turned(both).reshape(12, 32, 128) * sine).reshape(384, 128)
    high, low = split(both)
    right = table[384:512, 384:]
    hat = (mul(high, right, PLAIN) + mul(low, right, PLAIN)).reshape(12, 32, 128)

    row = lax.broadcasted_iota(jnp.int32, (32, 128), 0)
    lane = lax.broadcasted_iota(jnp.int32, (32, 128), 1)
    low_y = lane % 16
    kx = row + 32 * (lane // 16 % SLAB)
    plane = kz == 0
    ky = jnp.where(plane, low_y, 16 * half + low_y)
    wave_x = jnp.where(kx >= NX // 2, kx - NX, kx).astype(F32) * (1.0 / NX)
    wave_y = jnp.where(ky >= NY // 2, ky - NY, ky).astype(F32) * (1.0 / NY)
    kz_own = jnp.where(plane, jnp.where(half == 1, -HALF, 0), kz)
    wave_z = jnp.full((32, 128), kz_own, jnp.int32).astype(F32) * (1.0 / NZ)
    flip_x = jnp.where(kx == NX // 2, -wave_x, wave_x)
    flip_y = jnp.where(ky == NY // 2, -wave_y, wave_y)
    flip_z = jnp.where(jnp.full((32, 128), kz_own, jnp.int32) == -HALF, -wave_z, wave_z)
    special = jnp.logical_and(jnp.full((32, 128), kz, jnp.int32) == 0, low_y == 0)
    edge_y = jnp.full((32, 128), -0.5, F32)

    first, second = [], []
    for k in range(COMPS):
        a, b = hat[k], hat[k + COMPS]
        first.append(jnp.where(special, 0.5 * (a + b), a))
        second.append(jnp.where(special, 0.5 * (a - b), 0.0))
    parts = [
        green_stress(first, unit([wave_x, wave_y, wave_z])),
        green_stress(first, unit([flip_x, flip_y, flip_z])),
        green_stress(second, unit([wave_x, edge_y, wave_z])),
        green_stress(second, unit([flip_x, -edge_y, flip_z])),
    ]
    result = [0.5 * ((parts[0][k] + parts[1][k]) + (parts[2][k] + parts[3][k])) for k in range(COMPS)]

    high, low = split(jnp.concatenate(result, axis=0))
    inverse = table[512:640, 384:]
    value = mul(high, inverse, PLAIN) + mul(low, inverse, PLAIN)
    value = (value.reshape(6, 32, 128) * cosine - turned(value).reshape(6, 32, 128) * sine).reshape(192, 128)
    stacked = jnp.concatenate([value, turned(value)], axis=0)
    answer = dot3((table[384:640, :384], table[640:896, :384]), split(stacked))
    kind = lax.broadcasted_iota(jnp.int32, (256, 128), 0) % 8
    answer = jnp.where(kind == 6, rows, answer).reshape(32, 8, 128)
    for copy in range(out_ref.shape[1]):
        out_ref[:, copy] = answer


def local_kernel(orient_ref, kappa_ref, phase_ref, part_ref):
    step = pl.program_id(0)
    per_step = phase_ref.shape[0]
    for index in range(per_step):
        orient = orient_ref[step * per_step + index]
        kappa = [TIME_STEP * kappa_ref[d, orient] for d in range(3)]
        center = 1.0 - 2.0 * (kappa[0] + kappa[1] + kappa[2])
        for x in range(SLAB):
            p = phase_ref[index, x]
            if x == 0:
                beside = phase_ref[index, x + 1]
            elif x == SLAB - 1:
                beside = phase_ref[index, x - 1]
            else:
                beside = phase_ref[index, x - 1] + phase_ref[index, x + 1]
            moved = kappa[0] * beside
            moved = moved + kappa[1] * (pltpu.roll(p, 1, 0) + pltpu.roll(p, NY - 1, 0))
            moved = moved + kappa[2] * (pltpu.roll(p, 1, 1) + pltpu.roll(p, NZ - 1, 1))
            cubic = (6.0 * TIME_STEP) - (TIME_STEP * (4.0 - 2.0 * CROSS_COUPLING)) * p
            part_ref[index, x] = p * (center + p * cubic) + moved


def edges_kernel(place_ref, orient_ref, kappa_ref, *refs):
    planes, (low_out, high_out) = refs[:8], refs[8:]
    x = place_ref[2]
    direct = (x != 0, x != SLAB - 1)
    half = planes[0].shape[0]
    for variant in range(2 * half):
        kappa = TIME_STEP * kappa_ref[0, orient_ref[variant]]
        for side, out in enumerate((low_out, high_out)):
            near, relayed = planes[side * 4 + variant // half], planes[side * 4 + 2 + variant // half]
            out[variant] = kappa * jnp.where(direct[side], near[variant % half], relayed[variant % half])


def update_kernel(
    place_ref, family_ref, eps_ref, mine_ref, other_ref, table, phase_ref, low_hbm, high_hbm, part_hbm,
    next_ref, stress_ref, base, low_ref, high_ref, part_ref, sems,
):
    step = pl.program_id(0)
    per_step = next_ref.shape[0]

    def part_copy(index):
        rows = pl.ds(index * per_step, per_step)
        return pltpu.make_async_copy(part_hbm.at[rows], part_ref.at[rows], sems.at[index])

    edge_copies = [
        pltpu.make_async_copy(low_hbm, low_ref, sems.at[phase_ref.shape[0] // per_step]),
        pltpu.make_async_copy(high_hbm, high_ref, sems.at[phase_ref.shape[0] // per_step + 1]),
    ]

    @pl.when(step == 0)
    def _():
        for copy in edge_copies:
            copy.start()
        for index in range(phase_ref.shape[0] // per_step):
            part_copy(index).start()
        first = place_ref[0] == 0

        def line(k):
            mine = mine_ref[pl.ds(k, 128, stride=8), :]
            other = other_ref[pl.ds(k, 128, stride=8), :]
            return jnp.concatenate([jnp.where(first, mine, other), jnp.where(first, other, mine)], axis=1)

        lines = [line(k) for k in range(COMPS)]
        packed = dot3(split(jnp.concatenate([block[:8] for block in lines], axis=0)), (table[2], table[3]))
        along_y = dot3(split(jnp.concatenate(lines, axis=0)), (table[0], table[1]))
        top = lax.broadcasted_iota(jnp.int32, (8, 256), 0) == 0
        for k in range(COMPS):
            block = along_y[k * 128 : k * 128 + 128]
            head = jnp.where(top, packed[k * 8 : k * 8 + 8], block[:8])
            block = jnp.concatenate([head, block[8:]], axis=0)
            block = jnp.concatenate([block[:, :128], block[:, 128:]], axis=0)
            cells = dot3(split(block.T), (table[4], table[5]))
            stress_ref[k] = cells.reshape(SLAB, NY, NZ)
        base[...] = (TIME_STEP * (2.0 + 2.0 * CROSS_COUPLING * line(6))).reshape(SLAB, NY, NZ)
        for copy in edge_copies:
            copy.wait()

    part_copy(step).wait()
    for index in range(per_step):
        variant = step * per_step + index
        family = family_ref[variant]
        weight = [eps_ref[k, family] * (-TIME_STEP * (2.0 if k < 3 else 4.0)) for k in range(COMPS)]
        for x in range(SLAB):
            slope = base[x]
            for k in range(COMPS):
                slope = slope + weight[k] * stress_ref[k, x]
            value = part_ref[variant, x] - phase_ref[variant, x] * slope
            if x == 0:
                value = value + low_ref[variant]
            if x == SLAB - 1:
                value = value + high_ref[variant]
            next_ref[index, x] = value


def vmem():
    return pl.BlockSpec(memory_space=pltpu.VMEM)


def smem():
    return pl.BlockSpec(memory_space=pltpu.SMEM)


def device(x, y, z, core):
    return (y % 4 * 2 + z % 8 // 4) * 32 + x % 4 * 8 + z % 4 * 2 + core


def halo_routes(side, turn):
    first, second = [], []
    for y in range(4):
        for z in range(8):
            for core in range(2):
                for x in range(4):
                    if 0 <= x + side < 4:
                        target = device(x + side, y, z, core)
                    else:
                        row = y + (z >= 4) if side > 0 else y - (z < 4)
                        target = device(x + side, row, z + 3 * turn, core)
                    first.append((device(x, y, z, core), target))
                edge = 0 if side > 0 else 3
                second.append((device(edge, y, z, core), device(edge, y, z + turn, core)))
    return first, second


def limit(mib):
    return pltpu.CompilerParams(vmem_limit_bytes=mib << 20)


def step(phase_field, kappa_table, eps_table, orient_index, family_index):
    slabs = lax.axis_size("gx")
    groups = lax.axis_size("vert")
    runs = groups // 2
    variants = phase_field.shape[0]
    place = lax.axis_index("vert")
    core = (place % 2).astype(jnp.int32)
    kz_own = (lax.axis_index("gx") * runs + place // 2).astype(jnp.int32)
    place_arr = jnp.stack([core, kz_own, (lax.axis_index("gx") % SLAB).astype(jnp.int32)])
    eps_t, kappa_t = eps_table.T, kappa_table.T

    tz = z_table()
    ry, rp = y_tables()
    hbm = pl.BlockSpec(memory_space=pltpu.HBM)

    spread = jax.ShapeDtypeStruct((1024, 128), F32)
    plane = jax.ShapeDtypeStruct((variants // 2, NY, NZ), F32)
    keep, send, *planes = pl.pallas_call(
        sums_kernel,
        in_specs=[smem()] * 3 + [hbm] * 2,
        out_specs=[vmem()] * 6,
        out_shape=[spread] * 2 + [plane] * 4,
        scratch_shapes=[
            pltpu.VMEM(phase_field.shape, F32),
            pltpu.VMEM((6, 256, 256), BF16),
            pltpu.VMEM((COMPS * 128, NZ), F32),
            pltpu.VMEM((128, NZ), F32),
            pltpu.SemaphoreType.DMA((SLAB + 1,)),
        ],
        compiler_params=limit(24),
        cost_estimate=pl.CostEstimate(flops=10**8, bytes_accessed=9 << 20, transcendentals=0),
        name="sums",
    )(
        place_arr, family_index, eps_t, pltpu.with_memory_space_constraint(phase_field, pltpu.HBM),
        pltpu.with_memory_space_constraint(stacked_halves(tz, ry, rp), pltpu.HBM),
    )

    partner = [(i, i ^ 1) for i in range(groups)]
    same_core = [[g * groups + 2 * r + c for g in range(slabs) for r in range(runs)] for c in range(2)]

    def exchange(value):
        return lax.all_to_all(
            value, ("gx", "vert"), split_axis=0, concat_axis=0, axis_index_groups=same_core, tiled=True
        )

    received = lax.ppermute(send, "vert", partner)
    summed = keep + received
    both = ("gx", "vert")
    arrivals, relays = [], []
    for index, (side, turn) in enumerate(((1, 1), (1, -1), (-1, 1), (-1, -1))):
        first, second = halo_routes(side, turn)
        arrivals.append(lax.ppermute(planes[index], both, first))
        relays.append(lax.ppermute(arrivals[index], both, second))

    arrived = exchange(summed.reshape(128, 8, 128)).reshape(slabs, runs, 8, 128)

    answers = pl.pallas_call(
        spectral_kernel,
        in_specs=[smem()] + [vmem()] * 2,
        out_specs=vmem(),
        out_shape=jax.ShapeDtypeStruct((slabs, runs, 8, 128), F32),
        compiler_params=limit(12),
        cost_estimate=pl.CostEstimate(flops=10**8, bytes_accessed=4 << 20, transcendentals=0),
        name="spectral",
    )(place_arr, arrived, spectral_tables(*x_tables()))

    mine = exchange(answers.reshape(128, 8, 128)).reshape(1024, 128)
    other = lax.ppermute(mine, "vert", partner)

    edge_low, edge_high = pl.pallas_call(
        edges_kernel,
        in_specs=[smem()] * 3 + [vmem()] * 8,
        out_specs=[vmem()] * 2,
        out_shape=[jax.ShapeDtypeStruct((variants, NY, NZ), F32)] * 2,
        compiler_params=limit(4),
        cost_estimate=pl.CostEstimate(flops=10**6, bytes_accessed=3 << 20, transcendentals=0),
        name="edges",
    )(place_arr, orient_index, kappa_t, *arrivals[:2], *relays[:2], *arrivals[2:], *relays[2:])

    per_step = 2
    whole = pl.BlockSpec((per_step, SLAB, NY, NZ), lambda i: (i, 0, 0, 0))
    part = pl.pallas_call(
        local_kernel,
        grid=(variants // per_step,),
        in_specs=[smem()] * 2 + [whole],
        out_specs=whole,
        out_shape=jax.ShapeDtypeStruct(phase_field.shape, F32),
        compiler_params=limit(4),
        cost_estimate=pl.CostEstimate(flops=10**7, bytes_accessed=20 << 20, transcendentals=0),
        name="local",
    )(orient_index, kappa_t, pltpu.with_memory_space_constraint(phase_field, pltpu.HBM))

    phase_next, stress = pl.pallas_call(
        update_kernel,
        grid=(variants // per_step,),
        in_specs=[smem()] * 3 + [vmem()] * 4 + [hbm] * 3,
        out_specs=[whole, pl.BlockSpec((COMPS, SLAB, NY, NZ), lambda i: (0, 0, 0, 0))],
        out_shape=[
            jax.ShapeDtypeStruct(phase_field.shape, F32),
            jax.ShapeDtypeStruct((COMPS, SLAB, NY, NZ), F32),
        ],
        scratch_shapes=[
            pltpu.VMEM((SLAB, NY, NZ), F32),
            pltpu.VMEM((variants, NY, NZ), F32),
            pltpu.VMEM((variants, NY, NZ), F32),
            pltpu.VMEM(phase_field.shape, F32),
            pltpu.SemaphoreType.DMA((variants // per_step + 2,)),
        ],
        compiler_params=limit(26),
        cost_estimate=pl.CostEstimate(flops=10**8, bytes_accessed=12 << 20, transcendentals=0),
        name="update",
    )(
        place_arr, family_index, eps_t, mine, other,
        stacked_halves(np.linalg.inv(ry), np.linalg.inv(rp), np.linalg.inv(tz).T),
        phase_field, *(pltpu.with_memory_space_constraint(value, pltpu.HBM) for value in (edge_low, edge_high, part)),
    )
    return phase_next, stress


def solution(mesh):
    return jax.shard_map(
        step,
        mesh=mesh,
        in_specs=(P("vert", "gx", None, None), P(), P(), P("vert"), P("vert")),
        out_specs=(P("vert", "gx", None, None), P(None, "gx", None, None)),
        check_vma=False,
    )
```

```python
import jax
import jax.numpy as jnp
import numpy as np
from jax import lax
from jax.experimental import pallas as pl
from jax.experimental.pallas import tpu as pltpu
from jax.sharding import PartitionSpec as P


LAME_LAMBDA = 1.5
SHEAR_MOD = 1.0
TIME_STEP = 0.1
CROSS_COUPLING = 0.02
TENSOR_SLOTS = ((0, 5, 4), (5, 1, 3), (4, 3, 2))
VOIGT_PAIRS = ((0, 0), (1, 1), (2, 2), (1, 2), (0, 2), (0, 1))
F32 = jnp.float32
BF16 = jnp.bfloat16
NX, NY, NZ = 128, 32, 256
SLAB = 4
SLABS = 32
HALF = NZ // 2
COMPS = 6


def z_table():
    z = np.arange(NZ)
    kz = np.arange(HALF)
    angle = 2 * np.pi * (np.outer(kz, z) % NZ) / NZ
    imag = -np.sin(angle)
    imag[0] = (-1.0) ** z
    return np.concatenate([np.cos(angle), imag])


def y_tables():
    general = np.zeros((2, SLAB, NY, 2, 2, SLAB, 16))
    packed = np.zeros((2, SLAB, NY, 2, 2, SLAB, 16))
    y = np.arange(NY)
    for half in range(2):
        for low in range(16):
            angle = 2 * np.pi * ((16 * half + low) * y % NY) / NY
            plain = 2 * np.pi * (low * y % NY) / NY
            for x in range(SLAB):
                general[0, x, :, half, 0, x, low] = np.cos(angle)
                general[1, x, :, half, 0, x, low] = np.sin(angle)
                general[0, x, :, half, 1, x, low] = -np.sin(angle)
                general[1, x, :, half, 1, x, low] = np.cos(angle)
                packed[half, x, :, half, 0, x, low] = np.cos(plain)
                packed[half, x, :, half, 1, x, low] = -np.sin(plain) if low else (-1.0) ** y
    return general.reshape(256, 256), packed.reshape(256, 256)


def x_tables():
    slab = np.arange(SLABS)
    angle = 2 * np.pi * (np.outer(slab, slab) % SLABS) / SLABS
    cosine, sine = np.cos(angle), np.sin(angle)
    left = np.zeros((COMPS, SLABS, 2, SLABS, 8))
    back = np.zeros((SLABS, 8, 2, COMPS, SLABS))
    for comp in range(COMPS):
        left[comp, :, 0, :, comp] = cosine
        left[comp, :, 1, :, comp] = sine
        back[:, comp, 0, comp, :] = cosine / NX
        back[:, comp, 1, comp, :] = -sine / NX
    lane = np.arange(128)
    plane = lane // 16 % SLAB
    turn = 2 * np.pi * np.outer(slab, plane) / NX
    right = np.zeros((2, SLAB, 16, 2, SLAB, 16))
    for plane_in in range(SLAB):
        for plane_out in range(SLAB):
            theta = 2 * np.pi * (plane_in * plane_out % SLAB) / SLAB
            for low in range(16):
                right[0, plane_in, low, 0, plane_out, low] = np.round(np.cos(theta))
                right[1, plane_in, low, 0, plane_out, low] = np.round(np.sin(theta))
                right[0, plane_in, low, 1, plane_out, low] = -np.round(np.sin(theta))
                right[1, plane_in, low, 1, plane_out, low] = np.round(np.cos(theta))
    right = right.reshape(128, 128)
    return left.reshape(192, 512), back.reshape(256, 384), np.cos(turn), np.sin(turn), right, right.T.copy()


def halves_of(table):
    full = np.asarray(table, np.float32)
    high = full.astype(jnp.bfloat16)
    low = (table - high.astype(np.float64)).astype(jnp.bfloat16)
    return high, low


def stacked_halves(*tables):
    parts = [half for table in tables for half in halves_of(table)]
    return jnp.asarray(np.stack(parts))


def spectral_tables(left, back, tc, ts, right, right_t):
    packed = np.zeros((896, 512), jnp.bfloat16)
    left_high, left_low = halves_of(left)
    back_high, back_low = halves_of(back)
    packed[0:192], packed[192:384] = left_high, left_low
    packed[384:640, :384], packed[640:896, :384] = back_high, back_low
    packed[384:512, 384:], packed[512:640, 384:] = right, right_t
    for index, part in enumerate(halves_of(tc) + halves_of(ts)):
        packed[640 + 32 * index : 672 + 32 * index, 384:] = part
    return jnp.asarray(packed)


PLAIN = (((1,), (0,)), ((), ()))
RIGHT_T = (((1,), (1,)), ((), ()))


def split(value):
    high = value.astype(BF16)
    return high, (value - high.astype(F32)).astype(BF16)


def mul(a, b, dims):
    return lax.dot_general(a, b, dims, preferred_element_type=F32)


def dot3(left, right, dims=PLAIN):
    return mul(left[0], right[0], dims) + (mul(left[0], right[1], dims) + mul(left[1], right[0], dims))


def sums_kernel(
    place_ref, family_hbm, eps_hbm, phase_hbm, table_hbm,
    keep_ref, send_ref, last_ref, front_ref, far_ref, relay_ref, phase, table, eigen, square, family_ref, eps_ref, sems,
):
    variants = phase.shape[0]
    loads = [pltpu.make_async_copy(phase_hbm.at[:, x], phase.at[:, x], sems.at[x]) for x in range(SLAB)]
    loads.append(pltpu.make_async_copy(table_hbm, table, sems.at[SLAB]))
    small = [
        pltpu.make_async_copy(family_hbm, family_ref, sems.at[SLAB + 1]),
        pltpu.make_async_copy(eps_hbm, eps_ref, sems.at[SLAB + 2]),
    ]
    for load in small + loads:
        load.start()
    for load in small:
        load.wait()
    weight = [[eps_ref[k, family_ref[v]] for k in range(COMPS)] for v in range(variants)]
    for x in range(SLAB):
        loads[x].wait()

        def tile_sum(tile, carry, x=x):
            row = pl.multiple_of(tile * 8, 8)
            total = [None] * COMPS
            plain = None
            for v in range(variants):
                value = phase[v, x, pl.ds(row, 8), :]
                value = value * value
                plain = value if plain is None else plain + value
                for k in range(COMPS):
                    term = weight[v][k] * value
                    total[k] = term if total[k] is None else total[k] + term
            square[pl.ds(x * NY + row, 8), :] = plain
            for k in range(COMPS):
                eigen[pl.ds(k * 128 + x * NY + row, 8), :] = total[k]
            return carry

        lax.fori_loop(0, NY // 8, tile_sum, 0)
        if x in (0, SLAB - 1):
            (front_ref if x == 0 else last_ref)[...] = phase[:, x]
    forward = place_ref[2] == SLAB - 1
    for v in range(variants):
        target = far_ref if v < variants // 2 else relay_ref
        target[v % (variants // 2)] = jnp.where(forward, phase[v, SLAB - 1], phase[v, 0])
    loads[SLAB].wait()

    first = place_ref[0] == 0
    along_z = dot3((table[0], table[1]), split(eigen[...]), RIGHT_T)
    lines = []
    for k in range(COMPS):
        block = along_z[:, k * 128 : k * 128 + 128]
        lines.append(jnp.concatenate([block[:HALF], block[HALF:]], axis=1))
    packed_rows = jnp.concatenate([line[:8] for line in lines], axis=0)
    along_y = dot3(split(jnp.concatenate(lines, axis=0)), (table[2], table[3]))
    packed = dot3(split(packed_rows), (table[4], table[5]))
    top = lax.broadcasted_iota(jnp.int32, (8, 256), 0) == 0
    for k in range(COMPS):
        block = along_y[k * 128 : k * 128 + 128]
        head = jnp.where(top, packed[k * 8 : k * 8 + 8], block[:8])
        block = jnp.concatenate([head, block[8:]], axis=0)
        keep_ref[pl.ds(k, 128, stride=8), :] = jnp.where(first, block[:, :128], block[:, 128:])
        send_ref[pl.ds(k, 128, stride=8), :] = jnp.where(first, block[:, 128:], block[:, :128])
    sums = square[...]
    keep_ref[pl.ds(6, 128, stride=8), :] = jnp.where(first, sums[:, :128], sums[:, 128:])
    send_ref[pl.ds(6, 128, stride=8), :] = jnp.where(first, sums[:, 128:], sums[:, :128])
    empty = jnp.zeros((128, 128), F32)
    keep_ref[pl.ds(7, 128, stride=8), :] = empty
    send_ref[pl.ds(7, 128, stride=8), :] = empty


def green_stress(strain, normals):
    trace_strain = strain[0] + strain[1] + strain[2]
    stiffened = [
        LAME_LAMBDA * trace_strain + 2.0 * SHEAR_MOD * strain[number] if number < 3 else 2.0 * SHEAR_MOD * strain[number]
        for number in range(6)
    ]
    traction = [sum(stiffened[TENSOR_SLOTS[row][col]] * normals[col] for col in range(3)) for row in range(3)]
    normal_part = normals[0] * traction[0] + normals[1] * traction[1] + normals[2] * traction[2]
    coupling = (LAME_LAMBDA + SHEAR_MOD) / (LAME_LAMBDA + 2.0 * SHEAR_MOD)
    shifted = [(traction[row] - normals[row] * normal_part * coupling) * (1.0 / SHEAR_MOD) for row in range(3)]
    excess = [
        0.5 * (normals[a] * shifted[b] + normals[b] * shifted[a]) - strain[number]
        for number, (a, b) in enumerate(VOIGT_PAIRS)
    ]
    trace_excess = excess[0] + excess[1] + excess[2]
    return [
        LAME_LAMBDA * trace_excess + 2.0 * SHEAR_MOD * excess[number] if number < 3 else 2.0 * SHEAR_MOD * excess[number]
        for number in range(6)
    ]


def unit(wave):
    length_sq = wave[0] * wave[0] + wave[1] * wave[1] + wave[2] * wave[2]
    positive = length_sq > 0
    inverse = jnp.where(positive, lax.rsqrt(jnp.where(positive, length_sq, 1.0)), 0.0)
    return [part * inverse for part in wave]


def spectral_kernel(place_ref, in_ref, table, out_ref):
    half, kz = place_ref[0], place_ref[1]
    rows = ((in_ref[:, 0] + in_ref[:, 1]) + (in_ref[:, 2] + in_ref[:, 3])).reshape(256, 128)
    lane1 = lax.broadcasted_iota(jnp.int32, (1, 128), 1)
    sign = jnp.where(lane1 < 64, 1.0, -1.0).astype(F32)

    def turned(value):
        return pltpu.roll(value, 64, 1) * sign

    flipped = rows * sign
    stacked = jnp.concatenate(
        [
            jnp.concatenate([rows, flipped], axis=1),
            jnp.concatenate([turned(rows), turned(flipped)], axis=1),
        ],
        axis=0,
    )
    spread = dot3((table[0:192], table[192:384]), split(stacked))
    both = jnp.concatenate([spread[:, :128], spread[:, 128:]], axis=0)
    turns = table[640:768, 384:].astype(F32)
    cosine = (turns[0:32] + turns[32:64])[None]
    sine = (turns[64:96] + turns[96:128])[None]
    both = (both.reshape(12, 32, 128) * cosine + turned(both).reshape(12, 32, 128) * sine).reshape(384, 128)
    high, low = split(both)
    right = table[384:512, 384:]
    hat = (mul(high, right, PLAIN) + mul(low, right, PLAIN)).reshape(12, 32, 128)

    row = lax.broadcasted_iota(jnp.int32, (32, 128), 0)
    lane = lax.broadcasted_iota(jnp.int32, (32, 128), 1)
    low_y = lane % 16
    kx = row + 32 * (lane // 16 % SLAB)
    plane = kz == 0
    ky = jnp.where(plane, low_y, 16 * half + low_y)
    wave_x = jnp.where(kx >= NX // 2, kx - NX, kx).astype(F32) * (1.0 / NX)
    wave_y = jnp.where(ky >= NY // 2, ky - NY, ky).astype(F32) * (1.0 / NY)
    kz_own = jnp.where(plane, jnp.where(half == 1, -HALF, 0), kz)
    wave_z = jnp.full((32, 128), kz_own, jnp.int32).astype(F32) * (1.0 / NZ)
    flip_x = jnp.where(kx == NX // 2, -wave_x, wave_x)
    flip_y = jnp.where(ky == NY // 2, -wave_y, wave_y)
    flip_z = jnp.where(jnp.full((32, 128), kz_own, jnp.int32) == -HALF, -wave_z, wave_z)
    special = jnp.logical_and(jnp.full((32, 128), kz, jnp.int32) == 0, low_y == 0)
    edge_y = jnp.full((32, 128), -0.5, F32)

    first, second = [], []
    for k in range(COMPS):
        a, b = hat[k], hat[k + COMPS]
        first.append(jnp.where(special, 0.5 * (a + b), a))
        second.append(jnp.where(special, 0.5 * (a - b), 0.0))
    parts = [
        green_stress(first, unit([wave_x, wave_y, wave_z])),
        green_stress(first, unit([flip_x, flip_y, flip_z])),
        green_stress(second, unit([wave_x, edge_y, wave_z])),
        green_stress(second, unit([flip_x, -edge_y, flip_z])),
    ]
    result = [0.5 * ((parts[0][k] + parts[1][k]) + (parts[2][k] + parts[3][k])) for k in range(COMPS)]

    high, low = split(jnp.concatenate(result, axis=0))
    inverse = table[512:640, 384:]
    value = mul(high, inverse, PLAIN) + mul(low, inverse, PLAIN)
    value = (value.reshape(6, 32, 128) * cosine - turned(value).reshape(6, 32, 128) * sine).reshape(192, 128)
    stacked = jnp.concatenate([value, turned(value)], axis=0)
    answer = dot3((table[384:640, :384], table[640:896, :384]), split(stacked))
    kind = lax.broadcasted_iota(jnp.int32, (256, 128), 0) % 8
    answer = jnp.where(kind == 6, rows, answer).reshape(32, 8, 128)
    for copy in range(out_ref.shape[1]):
        out_ref[:, copy] = answer


def local_kernel(orient_ref, kappa_ref, phase_ref, part_ref):
    step = pl.program_id(0)
    per_step = phase_ref.shape[0]
    for index in range(per_step):
        orient = orient_ref[step * per_step + index]
        kappa = [TIME_STEP * kappa_ref[d, orient] for d in range(3)]
        center = 1.0 - 2.0 * (kappa[0] + kappa[1] + kappa[2])
        for x in range(SLAB):
            p = phase_ref[index, x]
            if x == 0:
                beside = phase_ref[index, x + 1]
            elif x == SLAB - 1:
                beside = phase_ref[index, x - 1]
            else:
                beside = phase_ref[index, x - 1] + phase_ref[index, x + 1]
            moved = kappa[0] * beside
            moved = moved + kappa[1] * (pltpu.roll(p, 1, 0) + pltpu.roll(p, NY - 1, 0))
            moved = moved + kappa[2] * (pltpu.roll(p, 1, 1) + pltpu.roll(p, NZ - 1, 1))
            cubic = (6.0 * TIME_STEP) - (TIME_STEP * (4.0 - 2.0 * CROSS_COUPLING)) * p
            part_ref[index, x] = p * (center + p * cubic) + moved


def edges_kernel(place_ref, orient_ref, kappa_ref, near_low, near_high, far, carried, low_out, high_out):
    x = place_ref[2]
    half = far.shape[0]
    for variant in range(2 * half):
        kappa = TIME_STEP * kappa_ref[0, orient_ref[variant]]
        remote = (far if variant < half else carried)[variant % half]
        low_out[variant] = kappa * jnp.where(x == 0, remote, near_low[variant])
        high_out[variant] = kappa * jnp.where(x == SLAB - 1, remote, near_high[variant])


def update_kernel(
    place_ref, family_ref, eps_ref, mine_ref, other_ref, table, phase_ref, low_hbm, high_hbm, part0, part1,
    next_ref, stress_ref, base, low_ref, high_ref, part_ref, sems,
):
    step = pl.program_id(0)
    per_step = next_ref.shape[0]

    count = phase_ref.shape[0] // per_step

    def part_start(index):
        source, at = (part0, index) if index < count // 2 else (part1, index - count // 2)
        rows, target = pl.ds(at * per_step, per_step), pl.ds(index * per_step, per_step)
        return pltpu.make_async_copy(source.at[rows], part_ref.at[target], sems.at[index])

    edge_copies = [
        pltpu.make_async_copy(low_hbm, low_ref, sems.at[count]),
        pltpu.make_async_copy(high_hbm, high_ref, sems.at[count + 1]),
    ]

    @pl.when(step == 0)
    def _():
        for copy in edge_copies:
            copy.start()
        for index in range(count):
            part_start(index).start()
        first = place_ref[0] == 0

        def line(k):
            mine = mine_ref[pl.ds(k, 128, stride=8), :]
            other = other_ref[pl.ds(k, 128, stride=8), :]
            return jnp.concatenate([jnp.where(first, mine, other), jnp.where(first, other, mine)], axis=1)

        lines = [line(k) for k in range(COMPS)]
        packed = dot3(split(jnp.concatenate([block[:8] for block in lines], axis=0)), (table[2], table[3]))
        along_y = dot3(split(jnp.concatenate(lines, axis=0)), (table[0], table[1]))
        top = lax.broadcasted_iota(jnp.int32, (8, 256), 0) == 0
        for k in range(COMPS):
            block = along_y[k * 128 : k * 128 + 128]
            head = jnp.where(top, packed[k * 8 : k * 8 + 8], block[:8])
            block = jnp.concatenate([head, block[8:]], axis=0)
            block = jnp.concatenate([block[:, :128], block[:, 128:]], axis=0)
            cells = dot3(split(block.T), (table[4], table[5]))
            stress_ref[k] = cells.reshape(SLAB, NY, NZ)
        base[...] = (TIME_STEP * (2.0 + 2.0 * CROSS_COUPLING * line(6))).reshape(SLAB, NY, NZ)
        for copy in edge_copies:
            copy.wait()

    rows = pl.ds(step * per_step, per_step)
    pltpu.make_async_copy(part0.at[pl.ds(0, per_step)], part_ref.at[rows], sems.at[step]).wait()
    for index in range(per_step):
        variant = step * per_step + index
        family = family_ref[variant]
        weight = [eps_ref[k, family] * (-TIME_STEP * (2.0 if k < 3 else 4.0)) for k in range(COMPS)]
        for x in range(SLAB):
            slope = base[x]
            for k in range(COMPS):
                slope = slope + weight[k] * stress_ref[k, x]
            value = part_ref[variant, x] - phase_ref[variant, x] * slope
            if x == 0:
                value = value + low_ref[variant]
            if x == SLAB - 1:
                value = value + high_ref[variant]
            next_ref[index, x] = value


def vmem():
    return pl.BlockSpec(memory_space=pltpu.VMEM)


def smem():
    return pl.BlockSpec(memory_space=pltpu.SMEM)


def device(x, y, z, core):
    return (y % 4 * 2 + z % 8 // 4) * 32 + x % 4 * 8 + z % 4 * 2 + core


def halo_routes():
    up, down, far, relay, carry = [], [], [], [], []
    for y in range(4):
        for z in range(8):
            for core in range(2):
                here = [device(x, y, z, core) for x in range(4)]
                after = device(0, y + (z >= 4), z + 4, core)
                before = device(3, y - (z < 4), z + 4, core)
                up += [(here[x], here[x + 1]) for x in range(3)]
                down += [(here[x + 1], here[x]) for x in range(3)]
                far += [(here[3], after), (here[0], before)]
                relay += [(here[3], here[2]), (here[0], here[1])]
                carry += [(here[2], after), (here[1], before)]
    return up, down, far, relay, carry


def in_hbm(value):
    return pltpu.with_memory_space_constraint(value, pltpu.HBM)


def limit(mib):
    return pltpu.CompilerParams(vmem_limit_bytes=mib << 20)


def step(phase_field, kappa_table, eps_table, orient_index, family_index):
    slabs = lax.axis_size("gx")
    groups = lax.axis_size("vert")
    runs = groups // 2
    variants = phase_field.shape[0]
    place = lax.axis_index("vert")
    core = (place % 2).astype(jnp.int32)
    kz_own = (lax.axis_index("gx") * runs + place // 2).astype(jnp.int32)
    place_arr = jnp.stack([core, kz_own, (lax.axis_index("gx") % SLAB).astype(jnp.int32)])
    eps_t, kappa_t = eps_table.T, kappa_table.T

    tz = z_table()
    ry, rp = y_tables()
    hbm = pl.BlockSpec(memory_space=pltpu.HBM)

    planes = [jax.ShapeDtypeStruct((count, NY, NZ), F32) for count in (variants, variants // 2)]
    spread = jax.ShapeDtypeStruct((1024, 128), F32)
    keep, send, last, front, far, relay = pl.pallas_call(
        sums_kernel,
        in_specs=[smem()] + [hbm] * 4,
        out_specs=[vmem()] * 6,
        out_shape=[spread] * 2 + [planes[0]] * 2 + [planes[1]] * 2,
        scratch_shapes=[
            pltpu.VMEM(phase_field.shape, F32),
            pltpu.VMEM((6, 256, 256), BF16),
            pltpu.VMEM((COMPS * 128, NZ), F32),
            pltpu.VMEM((128, NZ), F32),
            pltpu.SMEM(family_index.shape, jnp.int32),
            pltpu.SMEM(eps_t.shape, F32),
            pltpu.SemaphoreType.DMA((SLAB + 3,)),
        ],
        compiler_params=limit(24),
        cost_estimate=pl.CostEstimate(flops=10**8, bytes_accessed=9 << 20, transcendentals=0),
        name="sums",
    )(place_arr, *(in_hbm(value) for value in (family_index, eps_t, phase_field, stacked_halves(tz, ry, rp))))

    partner = [(i, i ^ 1) for i in range(groups)]
    same_core = [[g * groups + 2 * r + c for g in range(slabs) for r in range(runs)] for c in range(2)]

    def exchange(value):
        return lax.all_to_all(
            value, ("gx", "vert"), split_axis=0, concat_axis=0, axis_index_groups=same_core, tiled=True
        )

    received = lax.ppermute(send, "vert", partner)
    summed = keep + received
    both = ("gx", "vert")
    up, down, across, handed, carried = halo_routes()
    relay = lax.ppermute(relay, both, handed)
    near_low = lax.ppermute(last, both, up)
    near_high = lax.ppermute(front, both, down)
    far = lax.ppermute(far, both, across)
    carry = lax.ppermute(relay, both, carried)

    arrived = exchange(summed.reshape(128, 8, 128)).reshape(slabs, runs, 8, 128)

    answers = pl.pallas_call(
        spectral_kernel,
        in_specs=[smem()] + [vmem()] * 2,
        out_specs=vmem(),
        out_shape=jax.ShapeDtypeStruct((slabs, runs, 8, 128), F32),
        compiler_params=limit(12),
        cost_estimate=pl.CostEstimate(flops=10**8, bytes_accessed=4 << 20, transcendentals=0),
        name="spectral",
    )(place_arr, arrived, spectral_tables(*x_tables()))

    mine = exchange(answers.reshape(128, 8, 128)).reshape(1024, 128)
    other = lax.ppermute(mine, "vert", partner)

    edge_low, edge_high = pl.pallas_call(
        edges_kernel,
        in_specs=[smem()] * 3 + [vmem()] * 4,
        out_specs=[vmem()] * 2,
        out_shape=[pltpu.HBM((variants, NY, NZ), F32)] * 2,
        compiler_params=limit(4),
        cost_estimate=pl.CostEstimate(flops=10**6, bytes_accessed=3 << 20, transcendentals=0),
        name="edges",
    )(place_arr, orient_index, kappa_t, near_low, near_high, far, carry)

    per_step = 2
    whole = pl.BlockSpec((per_step, SLAB, NY, NZ), lambda i: (i, 0, 0, 0))
    half = variants // 2
    orients = [orient_index[:half], orient_index[half:]]
    part = []
    for index in range(2):
        part.append(
            pl.pallas_call(
                local_kernel,
                grid=(half // per_step,),
                in_specs=[
                    smem(),
                    smem(),
                    pl.BlockSpec(whole.block_shape, lambda i, at=index * half // per_step: (i + at, 0, 0, 0)),
                ],
                out_specs=whole,
                out_shape=pltpu.HBM((half, SLAB, NY, NZ), F32),
                compiler_params=limit(4),
                cost_estimate=pl.CostEstimate(flops=10**7, bytes_accessed=10 << 20, transcendentals=0),
            )(
                orients[index], kappa_t,
                in_hbm(phase_field),
            )
        )

    phase_next, stress = pl.pallas_call(
        update_kernel,
        grid=(variants // per_step,),
        in_specs=[smem()] * 3 + [vmem()] * 4 + [hbm] * 4,
        out_specs=[whole, pl.BlockSpec((COMPS, SLAB, NY, NZ), lambda i: (0, 0, 0, 0))],
        out_shape=[
            jax.ShapeDtypeStruct(phase_field.shape, F32),
            jax.ShapeDtypeStruct((COMPS, SLAB, NY, NZ), F32),
        ],
        scratch_shapes=[
            pltpu.VMEM((SLAB, NY, NZ), F32),
            pltpu.VMEM((variants, NY, NZ), F32),
            pltpu.VMEM((variants, NY, NZ), F32),
            pltpu.VMEM(phase_field.shape, F32),
            pltpu.SemaphoreType.DMA((variants // per_step + 2,)),
        ],
        compiler_params=limit(26),
        cost_estimate=pl.CostEstimate(flops=10**8, bytes_accessed=12 << 20, transcendentals=0),
        name="update",
    )(
        place_arr, family_index, eps_t, mine, other,
        stacked_halves(np.linalg.inv(ry), np.linalg.inv(rp), np.linalg.inv(tz).T),
        phase_field, *(in_hbm(value) for value in (edge_low, edge_high, *part)),
    )
    return phase_next, stress


def solution(mesh):
    return jax.shard_map(
        step,
        mesh=mesh,
        in_specs=(P("vert", "gx", None, None), P(), P(), P("vert"), P("vert")),
        out_specs=(P("vert", "gx", None, None), P(None, "gx", None, None)),
        check_vma=False,
    )
```

```python
import functools

import jax
import jax.numpy as jnp
import numpy as np
from jax import lax
from jax.experimental import pallas as pl
from jax.experimental.pallas import tpu as pltpu
from jax.sharding import PartitionSpec as P


LAME_LAMBDA = 1.5
SHEAR_MOD = 1.0
TIME_STEP = 0.1
CROSS_COUPLING = 0.02
TENSOR_SLOTS = ((0, 5, 4), (5, 1, 3), (4, 3, 2))
VOIGT_PAIRS = ((0, 0), (1, 1), (2, 2), (1, 2), (0, 2), (0, 1))
F32 = jnp.float32
BF16 = jnp.bfloat16
NX, NY, NZ = 128, 32, 256
SLAB = 4
SLABS = 32
HALF = NZ // 2
COMPS = 6


def z_table():
    z = np.arange(NZ)
    kz = np.arange(HALF)
    angle = 2 * np.pi * (np.outer(kz, z) % NZ) / NZ
    imag = -np.sin(angle)
    imag[0] = (-1.0) ** z
    return np.concatenate([np.cos(angle), imag])


def y_tables():
    general = np.zeros((2, SLAB, NY, 2, 2, SLAB, 16))
    packed = np.zeros((2, SLAB, NY, 2, 2, SLAB, 16))
    y = np.arange(NY)
    for half in range(2):
        for low in range(16):
            angle = 2 * np.pi * ((16 * half + low) * y % NY) / NY
            plain = 2 * np.pi * (low * y % NY) / NY
            for x in range(SLAB):
                general[0, x, :, half, 0, x, low] = np.cos(angle)
                general[1, x, :, half, 0, x, low] = np.sin(angle)
                general[0, x, :, half, 1, x, low] = -np.sin(angle)
                general[1, x, :, half, 1, x, low] = np.cos(angle)
                packed[half, x, :, half, 0, x, low] = np.cos(plain)
                packed[half, x, :, half, 1, x, low] = -np.sin(plain) if low else (-1.0) ** y
    return general.reshape(256, 256), packed.reshape(256, 256)


def x_tables():
    slab = np.arange(SLABS)
    angle = 2 * np.pi * (np.outer(slab, slab) % SLABS) / SLABS
    cosine, sine = np.cos(angle), np.sin(angle)
    left = np.zeros((COMPS, SLABS, 2, SLABS, 8))
    back = np.zeros((SLABS, 8, 2, COMPS, SLABS))
    for comp in range(COMPS):
        left[comp, :, 0, :, comp] = cosine
        left[comp, :, 1, :, comp] = sine
        back[:, comp, 0, comp, :] = cosine / NX
        back[:, comp, 1, comp, :] = -sine / NX
    lane = np.arange(128)
    plane = lane // 16 % SLAB
    turn = 2 * np.pi * np.outer(slab, plane) / NX
    right = np.zeros((2, SLAB, 16, 2, SLAB, 16))
    for plane_in in range(SLAB):
        for plane_out in range(SLAB):
            theta = 2 * np.pi * (plane_in * plane_out % SLAB) / SLAB
            for low in range(16):
                right[0, plane_in, low, 0, plane_out, low] = np.round(np.cos(theta))
                right[1, plane_in, low, 0, plane_out, low] = np.round(np.sin(theta))
                right[0, plane_in, low, 1, plane_out, low] = -np.round(np.sin(theta))
                right[1, plane_in, low, 1, plane_out, low] = np.round(np.cos(theta))
    right = right.reshape(128, 128)
    return left.reshape(192, 512), back.reshape(256, 384), np.cos(turn), np.sin(turn), right, right.T.copy()


def halves_of(table):
    full = np.asarray(table, np.float32)
    high = full.astype(jnp.bfloat16)
    low = (table - high.astype(np.float64)).astype(jnp.bfloat16)
    return high, low


def stacked_halves(*tables):
    parts = [half for table in tables for half in halves_of(table)]
    return jnp.asarray(np.stack(parts))


def spectral_tables(left, back, tc, ts, right, right_t):
    packed = np.zeros((896, 512), jnp.bfloat16)
    left_high, left_low = halves_of(left)
    back_high, back_low = halves_of(back)
    packed[0:192], packed[192:384] = left_high, left_low
    packed[384:640, :384], packed[640:896, :384] = back_high, back_low
    packed[384:512, 384:], packed[512:640, 384:] = right, right_t
    for index, part in enumerate(halves_of(tc) + halves_of(ts)):
        packed[640 + 32 * index : 672 + 32 * index, 384:] = part
    return jnp.asarray(packed)


PLAIN = (((1,), (0,)), ((), ()))
RIGHT_T = (((1,), (1,)), ((), ()))


def split(value):
    high = value.astype(BF16)
    return high, (value - high.astype(F32)).astype(BF16)


def mul(a, b, dims):
    return lax.dot_general(a, b, dims, preferred_element_type=F32)


def dot3(left, right, dims=PLAIN):
    return mul(left[0], right[0], dims) + (mul(left[0], right[1], dims) + mul(left[1], right[0], dims))


def sums_kernel(
    place_ref, family_hbm, eps_hbm, phase_hbm, table_hbm,
    keep_ref, send_ref, last_ref, front_ref, far_ref, relay_ref, phase, table, eigen, square, family_ref, eps_ref, sems,
):
    variants = phase.shape[0]
    loads = [pltpu.make_async_copy(phase_hbm.at[:, x], phase.at[:, x], sems.at[x]) for x in range(SLAB)]
    loads.append(pltpu.make_async_copy(table_hbm, table, sems.at[SLAB]))
    small = [
        pltpu.make_async_copy(family_hbm, family_ref, sems.at[SLAB + 1]),
        pltpu.make_async_copy(eps_hbm, eps_ref, sems.at[SLAB + 2]),
    ]
    for load in small + loads:
        load.start()
    for load in small:
        load.wait()
    weight = [[eps_ref[k, family_ref[v]] for k in range(COMPS)] for v in range(variants)]
    for x in range(SLAB):
        loads[x].wait()

        def tile_sum(tile, carry, x=x):
            row = pl.multiple_of(tile * 8, 8)
            total = [None] * COMPS
            plain = None
            for v in range(variants):
                value = phase[v, x, pl.ds(row, 8), :]
                value = value * value
                plain = value if plain is None else plain + value
                for k in range(COMPS):
                    term = weight[v][k] * value
                    total[k] = term if total[k] is None else total[k] + term
            square[pl.ds(x * NY + row, 8), :] = plain
            for k in range(COMPS):
                eigen[pl.ds(k * 128 + x * NY + row, 8), :] = total[k]
            return carry

        lax.fori_loop(0, NY // 8, tile_sum, 0)
        if x in (0, SLAB - 1):
            (front_ref if x == 0 else last_ref)[...] = phase[:, x]
    forward = place_ref[2] == SLAB - 1
    for v in range(variants):
        target = far_ref if v < variants // 2 else relay_ref
        target[v % (variants // 2)] = jnp.where(forward, phase[v, SLAB - 1], phase[v, 0])
    loads[SLAB].wait()

    first = place_ref[0] == 0
    along_z = dot3((table[0], table[1]), split(eigen[...]), RIGHT_T)
    lines = []
    for k in range(COMPS):
        block = along_z[:, k * 128 : k * 128 + 128]
        lines.append(jnp.concatenate([block[:HALF], block[HALF:]], axis=1))
    packed_rows = jnp.concatenate([line[:8] for line in lines], axis=0)
    along_y = dot3(split(jnp.concatenate(lines, axis=0)), (table[2], table[3]))
    packed = dot3(split(packed_rows), (table[4], table[5]))
    top = lax.broadcasted_iota(jnp.int32, (8, 256), 0) == 0
    for k in range(COMPS):
        block = along_y[k * 128 : k * 128 + 128]
        head = jnp.where(top, packed[k * 8 : k * 8 + 8], block[:8])
        block = jnp.concatenate([head, block[8:]], axis=0)
        keep_ref[pl.ds(k, 128, stride=8), :] = jnp.where(first, block[:, :128], block[:, 128:])
        send_ref[pl.ds(k, 128, stride=8), :] = jnp.where(first, block[:, 128:], block[:, :128])
    sums = square[...]
    keep_ref[pl.ds(6, 128, stride=8), :] = jnp.where(first, sums[:, :128], sums[:, 128:])
    send_ref[pl.ds(6, 128, stride=8), :] = jnp.where(first, sums[:, 128:], sums[:, :128])
    empty = jnp.zeros((128, 128), F32)
    keep_ref[pl.ds(7, 128, stride=8), :] = empty
    send_ref[pl.ds(7, 128, stride=8), :] = empty


def green_stress(strain, normals):
    trace_strain = strain[0] + strain[1] + strain[2]
    stiffened = [
        LAME_LAMBDA * trace_strain + 2.0 * SHEAR_MOD * strain[number] if number < 3 else 2.0 * SHEAR_MOD * strain[number]
        for number in range(6)
    ]
    traction = [sum(stiffened[TENSOR_SLOTS[row][col]] * normals[col] for col in range(3)) for row in range(3)]
    normal_part = normals[0] * traction[0] + normals[1] * traction[1] + normals[2] * traction[2]
    coupling = (LAME_LAMBDA + SHEAR_MOD) / (LAME_LAMBDA + 2.0 * SHEAR_MOD)
    shifted = [(traction[row] - normals[row] * normal_part * coupling) * (1.0 / SHEAR_MOD) for row in range(3)]
    excess = [
        0.5 * (normals[a] * shifted[b] + normals[b] * shifted[a]) - strain[number]
        for number, (a, b) in enumerate(VOIGT_PAIRS)
    ]
    trace_excess = excess[0] + excess[1] + excess[2]
    return [
        LAME_LAMBDA * trace_excess + 2.0 * SHEAR_MOD * excess[number] if number < 3 else 2.0 * SHEAR_MOD * excess[number]
        for number in range(6)
    ]


def unit(wave):
    length_sq = wave[0] * wave[0] + wave[1] * wave[1] + wave[2] * wave[2]
    positive = length_sq > 0
    inverse = jnp.where(positive, lax.rsqrt(jnp.where(positive, length_sq, 1.0)), 0.0)
    return [part * inverse for part in wave]


def spectral_kernel(place_ref, in_ref, table, out_ref):
    half, kz = place_ref[0], place_ref[1]
    rows = ((in_ref[0] + in_ref[1]) + (in_ref[2] + in_ref[3])).reshape(256, 128)
    lane1 = lax.broadcasted_iota(jnp.int32, (1, 128), 1)
    sign = jnp.where(lane1 < 64, 1.0, -1.0).astype(F32)

    def turned(value):
        return pltpu.roll(value, 64, 1) * sign

    flipped = rows * sign
    stacked = jnp.concatenate(
        [
            jnp.concatenate([rows, flipped], axis=1),
            jnp.concatenate([turned(rows), turned(flipped)], axis=1),
        ],
        axis=0,
    )
    spread = dot3((table[0:192], table[192:384]), split(stacked))
    both = jnp.concatenate([spread[:, :128], spread[:, 128:]], axis=0)
    turns = table[640:768, 384:].astype(F32)
    cosine = (turns[0:32] + turns[32:64])[None]
    sine = (turns[64:96] + turns[96:128])[None]
    both = (both.reshape(12, 32, 128) * cosine + turned(both).reshape(12, 32, 128) * sine).reshape(384, 128)
    high, low = split(both)
    right = table[384:512, 384:]
    hat = (mul(high, right, PLAIN) + mul(low, right, PLAIN)).reshape(12, 32, 128)

    row = lax.broadcasted_iota(jnp.int32, (32, 128), 0)
    lane = lax.broadcasted_iota(jnp.int32, (32, 128), 1)
    low_y = lane % 16
    kx = row + 32 * (lane // 16 % SLAB)
    plane = kz == 0
    ky = jnp.where(plane, low_y, 16 * half + low_y)
    wave_x = jnp.where(kx >= NX // 2, kx - NX, kx).astype(F32) * (1.0 / NX)
    wave_y = jnp.where(ky >= NY // 2, ky - NY, ky).astype(F32) * (1.0 / NY)
    kz_own = jnp.where(plane, jnp.where(half == 1, -HALF, 0), kz)
    wave_z = jnp.full((32, 128), kz_own, jnp.int32).astype(F32) * (1.0 / NZ)
    flip_x = jnp.where(kx == NX // 2, -wave_x, wave_x)
    flip_y = jnp.where(ky == NY // 2, -wave_y, wave_y)
    flip_z = jnp.where(jnp.full((32, 128), kz_own, jnp.int32) == -HALF, -wave_z, wave_z)
    special = jnp.logical_and(jnp.full((32, 128), kz, jnp.int32) == 0, low_y == 0)
    edge_y = jnp.full((32, 128), -0.5, F32)

    first, second = [], []
    for k in range(COMPS):
        a, b = hat[k], hat[k + COMPS]
        first.append(jnp.where(special, 0.5 * (a + b), a))
        second.append(jnp.where(special, 0.5 * (a - b), 0.0))
    parts = [
        green_stress(first, unit([wave_x, wave_y, wave_z])),
        green_stress(first, unit([flip_x, flip_y, flip_z])),
        green_stress(second, unit([wave_x, edge_y, wave_z])),
        green_stress(second, unit([flip_x, -edge_y, flip_z])),
    ]
    result = [0.5 * ((parts[0][k] + parts[1][k]) + (parts[2][k] + parts[3][k])) for k in range(COMPS)]

    high, low = split(jnp.concatenate(result, axis=0))
    inverse = table[512:640, 384:]
    value = mul(high, inverse, PLAIN) + mul(low, inverse, PLAIN)
    value = (value.reshape(6, 32, 128) * cosine - turned(value).reshape(6, 32, 128) * sine).reshape(192, 128)
    stacked = jnp.concatenate([value, turned(value)], axis=0)
    answer = dot3((table[384:640, :384], table[640:896, :384]), split(stacked))
    kind = lax.broadcasted_iota(jnp.int32, (256, 128), 0) % 8
    answer = jnp.where(kind == 6, rows, answer).reshape(32, 8, 128)
    for copy in range(out_ref.shape[0]):
        out_ref[copy] = answer


def local_kernel(orient_low, orient_high, kappa_ref, phase_ref, part_ref):
    half = orient_low.shape[0]

    def one(place, carry, orient_ref, at):
        orient = orient_ref[place]
        variant = place + at
        kappa = [TIME_STEP * kappa_ref[d, orient] for d in range(3)]
        center = 1.0 - 2.0 * (kappa[0] + kappa[1] + kappa[2])
        for x in range(SLAB):
            p = phase_ref[variant, x]
            if x == 0:
                beside = phase_ref[variant, x + 1]
            elif x == SLAB - 1:
                beside = phase_ref[variant, x - 1]
            else:
                beside = phase_ref[variant, x - 1] + phase_ref[variant, x + 1]
            moved = kappa[0] * beside
            moved = moved + kappa[1] * (pltpu.roll(p, 1, 0) + pltpu.roll(p, NY - 1, 0))
            moved = moved + kappa[2] * (pltpu.roll(p, 1, 1) + pltpu.roll(p, NZ - 1, 1))
            cubic = (6.0 * TIME_STEP) - (TIME_STEP * (4.0 - 2.0 * CROSS_COUPLING)) * p
            part_ref[variant, x] = p * (center + p * cubic) + moved
        return carry

    lax.fori_loop(0, half, functools.partial(one, orient_ref=orient_low, at=0), 0)
    lax.fori_loop(0, half, functools.partial(one, orient_ref=orient_high, at=half), 0)


def edges_kernel(place_ref, orient_ref, kappa_ref, near_low, near_high, far, carried, low_out, high_out):
    x = place_ref[2]
    half = far.shape[0]
    for variant in range(2 * half):
        kappa = TIME_STEP * kappa_ref[0, orient_ref[variant]]
        remote = (far if variant < half else carried)[variant % half]
        low_out[variant] = kappa * jnp.where(x == 0, remote, near_low[variant])
        high_out[variant] = kappa * jnp.where(x == SLAB - 1, remote, near_high[variant])


def update_kernel(
    place_ref, family_ref, eps_ref, mine_ref, other_ref, table, phase_ref, low_hbm, high_hbm, part_hbm,
    next_ref, stress_ref, base, low_ref, high_ref, part_ref, sems,
):
    step = pl.program_id(0)
    per_step = next_ref.shape[0]

    count = phase_ref.shape[0] // per_step

    def part_start(index):
        rows = pl.ds(index * per_step, per_step)
        return pltpu.make_async_copy(part_hbm.at[rows], part_ref.at[rows], sems.at[index])

    edge_copies = [
        pltpu.make_async_copy(low_hbm, low_ref, sems.at[count]),
        pltpu.make_async_copy(high_hbm, high_ref, sems.at[count + 1]),
    ]

    @pl.when(step == 0)
    def _():
        for copy in edge_copies:
            copy.start()
        for index in range(count):
            part_start(index).start()
        first = place_ref[0] == 0

        def line(k):
            mine = mine_ref[pl.ds(k, 128, stride=8), :]
            other = other_ref[pl.ds(k, 128, stride=8), :]
            return jnp.concatenate([jnp.where(first, mine, other), jnp.where(first, other, mine)], axis=1)

        lines = [line(k) for k in range(COMPS)]
        packed = dot3(split(jnp.concatenate([block[:8] for block in lines], axis=0)), (table[2], table[3]))
        along_y = dot3(split(jnp.concatenate(lines, axis=0)), (table[0], table[1]))
        top = lax.broadcasted_iota(jnp.int32, (8, 256), 0) == 0
        for k in range(COMPS):
            block = along_y[k * 128 : k * 128 + 128]
            head = jnp.where(top, packed[k * 8 : k * 8 + 8], block[:8])
            block = jnp.concatenate([head, block[8:]], axis=0)
            block = jnp.concatenate([block[:, :128], block[:, 128:]], axis=0)
            cells = dot3(split(block.T), (table[4], table[5]))
            stress_ref[k] = cells.reshape(SLAB, NY, NZ)
        base[...] = (TIME_STEP * (2.0 + 2.0 * CROSS_COUPLING * line(6))).reshape(SLAB, NY, NZ)
        for copy in edge_copies:
            copy.wait()

    rows = pl.ds(step * per_step, per_step)
    pltpu.make_async_copy(part_hbm.at[pl.ds(0, per_step)], part_ref.at[rows], sems.at[step]).wait()
    for index in range(per_step):
        variant = step * per_step + index
        family = family_ref[variant]
        weight = [eps_ref[k, family] * (-TIME_STEP * (2.0 if k < 3 else 4.0)) for k in range(COMPS)]
        for x in range(SLAB):
            slope = base[x]
            for k in range(COMPS):
                slope = slope + weight[k] * stress_ref[k, x]
            value = part_ref[variant, x] - phase_ref[variant, x] * slope
            if x == 0:
                value = value + low_ref[variant]
            if x == SLAB - 1:
                value = value + high_ref[variant]
            next_ref[index, x] = value


def vmem():
    return pl.BlockSpec(memory_space=pltpu.VMEM)


def smem():
    return pl.BlockSpec(memory_space=pltpu.SMEM)


def device(x, y, z, core):
    return (y % 4 * 2 + z % 8 // 4) * 32 + x % 4 * 8 + z % 4 * 2 + core


def halo_routes():
    up, down, far, relay, carry = [], [], [], [], []
    for y in range(4):
        for z in range(8):
            for core in range(2):
                here = [device(x, y, z, core) for x in range(4)]
                after = device(0, y + (z >= 4), z + 4, core)
                before = device(3, y - (z < 4), z + 4, core)
                up += [(here[x], here[x + 1]) for x in range(3)]
                down += [(here[x + 1], here[x]) for x in range(3)]
                far += [(here[3], after), (here[0], before)]
                relay += [(here[3], here[2]), (here[0], here[1])]
                carry += [(here[2], after), (here[1], before)]
    return up, down, far, relay, carry


def in_hbm(value):
    return pltpu.with_memory_space_constraint(value, pltpu.HBM)


def limit(mib):
    return pltpu.CompilerParams(vmem_limit_bytes=mib << 20)


def step(phase_field, kappa_table, eps_table, orient_index, family_index):
    slabs = lax.axis_size("gx")
    groups = lax.axis_size("vert")
    runs = groups // 2
    variants = phase_field.shape[0]
    place = lax.axis_index("vert")
    core = (place % 2).astype(jnp.int32)
    kz_own = (place // 2 * slabs + lax.axis_index("gx")).astype(jnp.int32)
    place_arr = jnp.stack([core, kz_own, (lax.axis_index("gx") % SLAB).astype(jnp.int32)])
    eps_t, kappa_t = eps_table.T, kappa_table.T

    tz = z_table()
    ry, rp = y_tables()
    hbm = pl.BlockSpec(memory_space=pltpu.HBM)

    planes = [pltpu.HBM((count, NY, NZ), F32) for count in (variants, variants // 2)]
    spread = jax.ShapeDtypeStruct((1024, 128), F32)
    keep, send, last, front, far, relay = pl.pallas_call(
        sums_kernel,
        in_specs=[smem()] + [hbm] * 4,
        out_specs=[vmem()] * 6,
        out_shape=[spread] * 2 + [planes[0]] * 2 + [planes[1]] * 2,
        scratch_shapes=[
            pltpu.VMEM(phase_field.shape, F32),
            pltpu.VMEM((6, 256, 256), BF16),
            pltpu.VMEM((COMPS * 128, NZ), F32),
            pltpu.VMEM((128, NZ), F32),
            pltpu.SMEM(family_index.shape, jnp.int32),
            pltpu.SMEM(eps_t.shape, F32),
            pltpu.SemaphoreType.DMA((SLAB + 3,)),
        ],
        compiler_params=limit(24),
        cost_estimate=pl.CostEstimate(flops=10**8, bytes_accessed=9 << 20, transcendentals=0),
        name="sums",
    )(place_arr, *(in_hbm(value) for value in (family_index, eps_t, phase_field, stacked_halves(tz, ry, rp))))

    partner = [(i, i ^ 1) for i in range(groups)]
    same_core = [[g * groups + 2 * r + c for r in range(runs) for g in range(slabs)] for c in range(2)]

    def exchange(value):
        return lax.all_to_all(
            value, ("gx", "vert"), split_axis=0, concat_axis=0, axis_index_groups=same_core, tiled=True
        )

    received = lax.ppermute(send, "vert", partner)
    summed = keep + received
    both = ("gx", "vert")
    up, down, across, handed, carried = halo_routes()
    relay = lax.ppermute(relay, both, handed)
    near_low = lax.ppermute(last, both, up)
    near_high = lax.ppermute(front, both, down)
    far = lax.ppermute(far, both, across)
    carry = lax.ppermute(relay, both, carried)

    arrived = exchange(summed.reshape(128, 8, 128)).reshape(runs, slabs, 8, 128)

    answers = pl.pallas_call(
        spectral_kernel,
        in_specs=[smem()] + [vmem()] * 2,
        out_specs=vmem(),
        out_shape=jax.ShapeDtypeStruct((runs, slabs, 8, 128), F32),
        compiler_params=limit(12),
        cost_estimate=pl.CostEstimate(flops=10**8, bytes_accessed=4 << 20, transcendentals=0),
        name="spectral",
    )(place_arr, arrived, spectral_tables(*x_tables()))

    mine = exchange(answers.reshape(128, 8, 128)).reshape(1024, 128)
    other = lax.ppermute(mine, "vert", partner)

    edge_low, edge_high = pl.pallas_call(
        edges_kernel,
        in_specs=[smem()] * 3 + [vmem()] * 4,
        out_specs=[vmem()] * 2,
        out_shape=[pltpu.HBM((variants, NY, NZ), F32)] * 2,
        compiler_params=limit(4),
        cost_estimate=pl.CostEstimate(flops=10**6, bytes_accessed=3 << 20, transcendentals=0),
        name="edges",
    )(place_arr, orient_index, kappa_t, near_low, near_high, far, carry)

    orients = [orient_index[: variants // 2], orient_index[variants // 2 :]]
    part = pl.pallas_call(
        local_kernel,
        in_specs=[smem()] * 3 + [vmem()],
        out_specs=vmem(),
        out_shape=pltpu.HBM(phase_field.shape, F32),
        compiler_params=limit(8),
        cost_estimate=pl.CostEstimate(flops=10**7, bytes_accessed=10 << 20, transcendentals=0),
        name="local",
    )(*orients, kappa_t, phase_field)

    per_step = 2
    whole = pl.BlockSpec((per_step, SLAB, NY, NZ), lambda i: (i, 0, 0, 0))
    phase_next, stress = pl.pallas_call(
        update_kernel,
        grid=(variants // per_step,),
        in_specs=[smem()] * 3 + [vmem()] * 4 + [hbm] * 3,
        out_specs=[whole, pl.BlockSpec((COMPS, SLAB, NY, NZ), lambda i: (0, 0, 0, 0))],
        out_shape=[
            jax.ShapeDtypeStruct(phase_field.shape, F32),
            jax.ShapeDtypeStruct((COMPS, SLAB, NY, NZ), F32),
        ],
        scratch_shapes=[
            pltpu.VMEM((SLAB, NY, NZ), F32),
            pltpu.VMEM((variants, NY, NZ), F32),
            pltpu.VMEM((variants, NY, NZ), F32),
            pltpu.VMEM(phase_field.shape, F32),
            pltpu.SemaphoreType.DMA((variants // per_step + 2,)),
        ],
        compiler_params=limit(26),
        cost_estimate=pl.CostEstimate(flops=10**8, bytes_accessed=12 << 20, transcendentals=0),
        name="update",
    )(
        place_arr, family_index, eps_t, mine, other,
        stacked_halves(np.linalg.inv(ry), np.linalg.inv(rp), np.linalg.inv(tz).T),
        phase_field, *(in_hbm(value) for value in (edge_low, edge_high, part)),
    )
    return phase_next, stress


def solution(mesh):
    return jax.shard_map(
        step,
        mesh=mesh,
        in_specs=(P("vert", "gx", None, None), P(), P(), P("vert"), P("vert")),
        out_specs=(P("vert", "gx", None, None), P(None, "gx", None, None)),
        check_vma=False,
    )
```

```python
import functools

import jax
import jax.numpy as jnp
import numpy as np
from jax import lax
from jax.experimental import pallas as pl
from jax.experimental.pallas import tpu as pltpu
from jax.sharding import PartitionSpec as P


LAME_LAMBDA = 1.5
SHEAR_MOD = 1.0
TIME_STEP = 0.1
CROSS_COUPLING = 0.02
TENSOR_SLOTS = ((0, 5, 4), (5, 1, 3), (4, 3, 2))
VOIGT_PAIRS = ((0, 0), (1, 1), (2, 2), (1, 2), (0, 2), (0, 1))
F32 = jnp.float32
BF16 = jnp.bfloat16
NX, NY, NZ = 128, 32, 256
SLAB = 4
SLABS = 32
HALF = NZ // 2
COMPS = 6
MEMBERS = [(0, 0), (8, 0), (16, 0), (24, 0), (1, 0), (9, 0), (17, 0), (25, 0), (2, 0), (10, 0), (18, 0), (26, 0), (3, 0), (11, 0), (19, 0), (27, 0), (4, 0), (12, 0), (20, 0), (28, 0), (5, 0), (13, 0), (21, 0), (29, 0), (6, 0), (14, 0), (22, 0), (30, 0), (7, 0), (15, 0), (23, 0), (31, 0), (0, 1), (8, 1), (16, 1), (24, 1), (1, 1), (9, 1), (17, 1), (25, 1), (2, 1), (10, 1), (18, 1), (26, 1), (3, 1), (11, 1), (19, 1), (27, 1), (4, 1), (12, 1), (20, 1), (28, 1), (5, 1), (13, 1), (21, 1), (29, 1), (6, 1), (14, 1), (22, 1), (30, 1), (7, 1), (15, 1), (23, 1), (31, 1), (0, 2), (8, 2), (16, 2), (24, 2), (1, 2), (9, 2), (17, 2), (25, 2), (2, 2), (10, 2), (18, 2), (26, 2), (3, 2), (11, 2), (19, 2), (27, 2), (4, 2), (12, 2), (20, 2), (28, 2), (5, 2), (13, 2), (21, 2), (29, 2), (6, 2), (14, 2), (22, 2), (30, 2), (7, 2), (15, 2), (23, 2), (31, 2), (0, 3), (8, 3), (16, 3), (24, 3), (1, 3), (9, 3), (17, 3), (25, 3), (2, 3), (10, 3), (18, 3), (26, 3), (3, 3), (11, 3), (19, 3), (27, 3), (4, 3), (12, 3), (20, 3), (28, 3), (5, 3), (13, 3), (21, 3), (29, 3), (6, 3), (14, 3), (22, 3), (30, 3), (7, 3), (15, 3), (23, 3), (31, 3)]
ROW_SLABS = [0, 8, 16, 24, 1, 9, 17, 25, 2, 10, 18, 26, 3, 11, 19, 27, 4, 12, 20, 28, 5, 13, 21, 29, 6, 14, 22, 30, 7, 15, 23, 31]


def z_table():
    z = np.arange(NZ)
    kz = np.arange(HALF)
    angle = 2 * np.pi * (np.outer(kz, z) % NZ) / NZ
    imag = -np.sin(angle)
    imag[0] = (-1.0) ** z
    return np.concatenate([np.cos(angle), imag])


def y_tables():
    general = np.zeros((2, SLAB, NY, 2, 2, SLAB, 16))
    packed = np.zeros((2, SLAB, NY, 2, 2, SLAB, 16))
    y = np.arange(NY)
    for half in range(2):
        for low in range(16):
            angle = 2 * np.pi * ((16 * half + low) * y % NY) / NY
            plain = 2 * np.pi * (low * y % NY) / NY
            for x in range(SLAB):
                general[0, x, :, half, 0, x, low] = np.cos(angle)
                general[1, x, :, half, 0, x, low] = np.sin(angle)
                general[0, x, :, half, 1, x, low] = -np.sin(angle)
                general[1, x, :, half, 1, x, low] = np.cos(angle)
                packed[half, x, :, half, 0, x, low] = np.cos(plain)
                packed[half, x, :, half, 1, x, low] = -np.sin(plain) if low else (-1.0) ** y
    return general.reshape(256, 256), packed.reshape(256, 256)


def x_tables():
    slab = np.arange(SLABS)
    angle = 2 * np.pi * (np.outer(slab, slab) % SLABS) / SLABS
    cosine, sine = np.cos(angle), np.sin(angle)
    left = np.zeros((COMPS, SLABS, 2, SLABS, 8))
    back = np.zeros((SLABS, 8, 2, COMPS, SLABS))
    for comp in range(COMPS):
        left[comp, :, 0, :, comp] = cosine
        left[comp, :, 1, :, comp] = sine
        back[:, comp, 0, comp, :] = cosine / NX
        back[:, comp, 1, comp, :] = -sine / NX
    lane = np.arange(128)
    plane = lane // 16 % SLAB
    turn = 2 * np.pi * np.outer(slab, plane) / NX
    right = np.zeros((2, SLAB, 16, 2, SLAB, 16))
    for plane_in in range(SLAB):
        for plane_out in range(SLAB):
            theta = 2 * np.pi * (plane_in * plane_out % SLAB) / SLAB
            for low in range(16):
                right[0, plane_in, low, 0, plane_out, low] = np.round(np.cos(theta))
                right[1, plane_in, low, 0, plane_out, low] = np.round(np.sin(theta))
                right[0, plane_in, low, 1, plane_out, low] = -np.round(np.sin(theta))
                right[1, plane_in, low, 1, plane_out, low] = np.round(np.cos(theta))
    left, back = left[..., ROW_SLABS, :], back[ROW_SLABS]
    right = right.reshape(128, 128)
    return left.reshape(192, 512), back.reshape(256, 384), np.cos(turn), np.sin(turn), right, right.T.copy()


def halves_of(table):
    full = np.asarray(table, np.float32)
    high = full.astype(jnp.bfloat16)
    low = (table - high.astype(np.float64)).astype(jnp.bfloat16)
    return high, low


def stacked_halves(*tables):
    parts = [half for table in tables for half in halves_of(table)]
    return jnp.asarray(np.stack(parts))


def spectral_tables(left, back, tc, ts, right, right_t):
    packed = np.zeros((896, 512), jnp.bfloat16)
    left_high, left_low = halves_of(left)
    back_high, back_low = halves_of(back)
    packed[0:192], packed[192:384] = left_high, left_low
    packed[384:640, :384], packed[640:896, :384] = back_high, back_low
    packed[384:512, 384:], packed[512:640, 384:] = right, right_t
    for index, part in enumerate(halves_of(tc) + halves_of(ts)):
        packed[640 + 32 * index : 672 + 32 * index, 384:] = part
    return jnp.asarray(packed)


PLAIN = (((1,), (0,)), ((), ()))
RIGHT_T = (((1,), (1,)), ((), ()))


def split(value):
    high = value.astype(BF16)
    return high, (value - high.astype(F32)).astype(BF16)


def mul(a, b, dims):
    return lax.dot_general(a, b, dims, preferred_element_type=F32)


def dot3(left, right, dims=PLAIN):
    return mul(left[0], right[0], dims) + (mul(left[0], right[1], dims) + mul(left[1], right[0], dims))


def sums_kernel(
    place_ref, family_hbm, eps_hbm, phase_hbm, table_hbm,
    keep_ref, send_ref, last_ref, front_ref, far_ref, relay_ref, phase, table, eigen, square, family_ref, eps_ref, sems,
):
    variants = phase.shape[0]
    loads = [pltpu.make_async_copy(phase_hbm.at[:, x], phase.at[:, x], sems.at[x]) for x in range(SLAB)]
    loads.append(pltpu.make_async_copy(table_hbm, table, sems.at[SLAB]))
    small = [
        pltpu.make_async_copy(family_hbm, family_ref, sems.at[SLAB + 1]),
        pltpu.make_async_copy(eps_hbm, eps_ref, sems.at[SLAB + 2]),
    ]
    for load in small + loads:
        load.start()
    for load in small:
        load.wait()
    weight = [[eps_ref[k, family_ref[v]] for k in range(COMPS)] for v in range(variants)]
    for x in range(SLAB):
        loads[x].wait()

        def tile_sum(tile, carry, x=x):
            row = pl.multiple_of(tile * 8, 8)
            total = [None] * COMPS
            plain = None
            for v in range(variants):
                value = phase[v, x, pl.ds(row, 8), :]
                value = value * value
                plain = value if plain is None else plain + value
                for k in range(COMPS):
                    term = weight[v][k] * value
                    total[k] = term if total[k] is None else total[k] + term
            square[pl.ds(x * NY + row, 8), :] = plain
            for k in range(COMPS):
                eigen[pl.ds(k * 128 + x * NY + row, 8), :] = total[k]
            return carry

        lax.fori_loop(0, NY // 8, tile_sum, 0)
        if x in (0, SLAB - 1):
            (front_ref if x == 0 else last_ref)[...] = phase[:, x]
    forward = place_ref[2] == SLAB - 1
    for v in range(variants):
        target = far_ref if v < variants // 2 else relay_ref
        target[v % (variants // 2)] = jnp.where(forward, phase[v, SLAB - 1], phase[v, 0])
    loads[SLAB].wait()

    first = place_ref[0] == 0
    along_z = dot3((table[0], table[1]), split(eigen[...]), RIGHT_T)
    lines = []
    for k in range(COMPS):
        block = along_z[:, k * 128 : k * 128 + 128]
        lines.append(jnp.concatenate([block[:HALF], block[HALF:]], axis=1))
    packed_rows = jnp.concatenate([line[:8] for line in lines], axis=0)
    along_y = dot3(split(jnp.concatenate(lines, axis=0)), (table[2], table[3]))
    packed = dot3(split(packed_rows), (table[4], table[5]))
    top = lax.broadcasted_iota(jnp.int32, (8, 256), 0) == 0
    for k in range(COMPS):
        block = along_y[k * 128 : k * 128 + 128]
        head = jnp.where(top, packed[k * 8 : k * 8 + 8], block[:8])
        block = jnp.concatenate([head, block[8:]], axis=0)
        keep_ref[pl.ds(k, 128, stride=8), :] = jnp.where(first, block[:, :128], block[:, 128:])
        send_ref[pl.ds(k, 128, stride=8), :] = jnp.where(first, block[:, 128:], block[:, :128])
    sums = square[...]
    keep_ref[pl.ds(6, 128, stride=8), :] = jnp.where(first, sums[:, :128], sums[:, 128:])
    send_ref[pl.ds(6, 128, stride=8), :] = jnp.where(first, sums[:, 128:], sums[:, :128])
    empty = jnp.zeros((128, 128), F32)
    keep_ref[pl.ds(7, 128, stride=8), :] = empty
    send_ref[pl.ds(7, 128, stride=8), :] = empty


def green_stress(strain, normals):
    trace_strain = strain[0] + strain[1] + strain[2]
    stiffened = [
        LAME_LAMBDA * trace_strain + 2.0 * SHEAR_MOD * strain[number] if number < 3 else 2.0 * SHEAR_MOD * strain[number]
        for number in range(6)
    ]
    traction = [sum(stiffened[TENSOR_SLOTS[row][col]] * normals[col] for col in range(3)) for row in range(3)]
    normal_part = normals[0] * traction[0] + normals[1] * traction[1] + normals[2] * traction[2]
    coupling = (LAME_LAMBDA + SHEAR_MOD) / (LAME_LAMBDA + 2.0 * SHEAR_MOD)
    shifted = [(traction[row] - normals[row] * normal_part * coupling) * (1.0 / SHEAR_MOD) for row in range(3)]
    excess = [
        0.5 * (normals[a] * shifted[b] + normals[b] * shifted[a]) - strain[number]
        for number, (a, b) in enumerate(VOIGT_PAIRS)
    ]
    trace_excess = excess[0] + excess[1] + excess[2]
    return [
        LAME_LAMBDA * trace_excess + 2.0 * SHEAR_MOD * excess[number] if number < 3 else 2.0 * SHEAR_MOD * excess[number]
        for number in range(6)
    ]


def unit(wave):
    length_sq = wave[0] * wave[0] + wave[1] * wave[1] + wave[2] * wave[2]
    positive = length_sq > 0
    inverse = jnp.where(positive, lax.rsqrt(jnp.where(positive, length_sq, 1.0)), 0.0)
    return [part * inverse for part in wave]


def spectral_kernel(place_ref, in_ref, table, out_ref):
    half, kz = place_ref[0], place_ref[1]
    rows = ((in_ref[:, 0] + in_ref[:, 1]) + (in_ref[:, 2] + in_ref[:, 3])).reshape(256, 128)
    lane1 = lax.broadcasted_iota(jnp.int32, (1, 128), 1)
    sign = jnp.where(lane1 < 64, 1.0, -1.0).astype(F32)

    def turned(value):
        return pltpu.roll(value, 64, 1) * sign

    flipped = rows * sign
    stacked = jnp.concatenate(
        [
            jnp.concatenate([rows, flipped], axis=1),
            jnp.concatenate([turned(rows), turned(flipped)], axis=1),
        ],
        axis=0,
    )
    spread = dot3((table[0:192], table[192:384]), split(stacked))
    both = jnp.concatenate([spread[:, :128], spread[:, 128:]], axis=0)
    turns = table[640:768, 384:].astype(F32)
    cosine = (turns[0:32] + turns[32:64])[None]
    sine = (turns[64:96] + turns[96:128])[None]
    both = (both.reshape(12, 32, 128) * cosine + turned(both).reshape(12, 32, 128) * sine).reshape(384, 128)
    high, low = split(both)
    right = table[384:512, 384:]
    hat = (mul(high, right, PLAIN) + mul(low, right, PLAIN)).reshape(12, 32, 128)

    row = lax.broadcasted_iota(jnp.int32, (32, 128), 0)
    lane = lax.broadcasted_iota(jnp.int32, (32, 128), 1)
    low_y = lane % 16
    kx = row + 32 * (lane // 16 % SLAB)
    plane = kz == 0
    ky = jnp.where(plane, low_y, 16 * half + low_y)
    wave_x = jnp.where(kx >= NX // 2, kx - NX, kx).astype(F32) * (1.0 / NX)
    wave_y = jnp.where(ky >= NY // 2, ky - NY, ky).astype(F32) * (1.0 / NY)
    kz_own = jnp.where(plane, jnp.where(half == 1, -HALF, 0), kz)
    wave_z = jnp.full((32, 128), kz_own, jnp.int32).astype(F32) * (1.0 / NZ)
    flip_x = jnp.where(kx == NX // 2, -wave_x, wave_x)
    flip_y = jnp.where(ky == NY // 2, -wave_y, wave_y)
    flip_z = jnp.where(jnp.full((32, 128), kz_own, jnp.int32) == -HALF, -wave_z, wave_z)
    special = jnp.logical_and(jnp.full((32, 128), kz, jnp.int32) == 0, low_y == 0)
    edge_y = jnp.full((32, 128), -0.5, F32)

    first, second = [], []
    for k in range(COMPS):
        a, b = hat[k], hat[k + COMPS]
        first.append(jnp.where(special, 0.5 * (a + b), a))
        second.append(jnp.where(special, 0.5 * (a - b), 0.0))
    parts = [
        green_stress(first, unit([wave_x, wave_y, wave_z])),
        green_stress(first, unit([flip_x, flip_y, flip_z])),
        green_stress(second, unit([wave_x, edge_y, wave_z])),
        green_stress(second, unit([flip_x, -edge_y, flip_z])),
    ]
    result = [0.5 * ((parts[0][k] + parts[1][k]) + (parts[2][k] + parts[3][k])) for k in range(COMPS)]

    high, low = split(jnp.concatenate(result, axis=0))
    inverse = table[512:640, 384:]
    value = mul(high, inverse, PLAIN) + mul(low, inverse, PLAIN)
    value = (value.reshape(6, 32, 128) * cosine - turned(value).reshape(6, 32, 128) * sine).reshape(192, 128)
    stacked = jnp.concatenate([value, turned(value)], axis=0)
    answer = dot3((table[384:640, :384], table[640:896, :384]), split(stacked))
    kind = lax.broadcasted_iota(jnp.int32, (256, 128), 0) % 8
    answer = jnp.where(kind == 6, rows, answer).reshape(out_ref.shape[0], out_ref.shape[2], 8, 128)
    for copy in range(out_ref.shape[1]):
        out_ref[:, copy] = answer


def local_kernel(orient_low, orient_high, kappa_ref, phase_ref, part_ref):
    half = orient_low.shape[0]

    def one(place, carry, orient_ref, at):
        orient = orient_ref[place]
        variant = place + at
        kappa = [TIME_STEP * kappa_ref[d, orient] for d in range(3)]
        center = 1.0 - 2.0 * (kappa[0] + kappa[1] + kappa[2])
        for x in range(SLAB):
            p = phase_ref[variant, x]
            if x == 0:
                beside = phase_ref[variant, x + 1]
            elif x == SLAB - 1:
                beside = phase_ref[variant, x - 1]
            else:
                beside = phase_ref[variant, x - 1] + phase_ref[variant, x + 1]
            moved = kappa[0] * beside
            moved = moved + kappa[1] * (pltpu.roll(p, 1, 0) + pltpu.roll(p, NY - 1, 0))
            moved = moved + kappa[2] * (pltpu.roll(p, 1, 1) + pltpu.roll(p, NZ - 1, 1))
            cubic = (6.0 * TIME_STEP) - (TIME_STEP * (4.0 - 2.0 * CROSS_COUPLING)) * p
            part_ref[variant, x] = p * (center + p * cubic) + moved
        return carry

    lax.fori_loop(0, half, functools.partial(one, orient_ref=orient_low, at=0), 0)
    lax.fori_loop(0, half, functools.partial(one, orient_ref=orient_high, at=half), 0)


def edges_kernel(place_ref, orient_ref, kappa_ref, near_low, near_high, far, carried, low_out, high_out):
    x = place_ref[2]
    half = far.shape[0]
    for variant in range(2 * half):
        kappa = TIME_STEP * kappa_ref[0, orient_ref[variant]]
        remote = (far if variant < half else carried)[variant % half]
        low_out[variant] = kappa * jnp.where(x == 0, remote, near_low[variant])
        high_out[variant] = kappa * jnp.where(x == SLAB - 1, remote, near_high[variant])


def update_kernel(
    place_ref, family_ref, eps_ref, mine_ref, other_ref, table, phase_ref, low_hbm, high_hbm, part_hbm,
    next_ref, stress_ref, base, low_ref, high_ref, part_ref, sems,
):
    step = pl.program_id(0)
    per_step = next_ref.shape[0]

    count = phase_ref.shape[0] // per_step

    def part_start(index):
        rows = pl.ds(index * per_step, per_step)
        return pltpu.make_async_copy(part_hbm.at[rows], part_ref.at[rows], sems.at[index])

    edge_copies = [
        pltpu.make_async_copy(low_hbm, low_ref, sems.at[count]),
        pltpu.make_async_copy(high_hbm, high_ref, sems.at[count + 1]),
    ]

    @pl.when(step == 0)
    def _():
        for copy in edge_copies:
            copy.start()
        for index in range(count):
            part_start(index).start()
        first = place_ref[0] == 0

        def line(k):
            mine = mine_ref[pl.ds(k, 128, stride=8), :]
            other = other_ref[pl.ds(k, 128, stride=8), :]
            return jnp.concatenate([jnp.where(first, mine, other), jnp.where(first, other, mine)], axis=1)

        lines = [line(k) for k in range(COMPS)]
        packed = dot3(split(jnp.concatenate([block[:8] for block in lines], axis=0)), (table[2], table[3]))
        along_y = dot3(split(jnp.concatenate(lines, axis=0)), (table[0], table[1]))
        top = lax.broadcasted_iota(jnp.int32, (8, 256), 0) == 0
        for k in range(COMPS):
            block = along_y[k * 128 : k * 128 + 128]
            head = jnp.where(top, packed[k * 8 : k * 8 + 8], block[:8])
            block = jnp.concatenate([head, block[8:]], axis=0)
            block = jnp.concatenate([block[:, :128], block[:, 128:]], axis=0)
            cells = dot3(split(block.T), (table[4], table[5]))
            stress_ref[k] = cells.reshape(SLAB, NY, NZ)
        base[...] = (TIME_STEP * (2.0 + 2.0 * CROSS_COUPLING * line(6))).reshape(SLAB, NY, NZ)
        for copy in edge_copies:
            copy.wait()

    rows = pl.ds(step * per_step, per_step)
    pltpu.make_async_copy(part_hbm.at[pl.ds(0, per_step)], part_ref.at[rows], sems.at[step]).wait()
    for index in range(per_step):
        variant = step * per_step + index
        family = family_ref[variant]
        weight = [eps_ref[k, family] * (-TIME_STEP * (2.0 if k < 3 else 4.0)) for k in range(COMPS)]
        for x in range(SLAB):
            slope = base[x]
            for k in range(COMPS):
                slope = slope + weight[k] * stress_ref[k, x]
            value = part_ref[variant, x] - phase_ref[variant, x] * slope
            if x == 0:
                value = value + low_ref[variant]
            if x == SLAB - 1:
                value = value + high_ref[variant]
            next_ref[index, x] = value


def vmem():
    return pl.BlockSpec(memory_space=pltpu.VMEM)


def smem():
    return pl.BlockSpec(memory_space=pltpu.SMEM)


def device(x, y, z, core):
    return (y % 4 * 2 + z % 8 // 4) * 32 + x % 4 * 8 + z % 4 * 2 + core


def halo_routes():
    up, down, far, relay, carry = [], [], [], [], []
    for y in range(4):
        for z in range(8):
            for core in range(2):
                here = [device(x, y, z, core) for x in range(4)]
                after = device(0, y + (z >= 4), z + 4, core)
                before = device(3, y - (z < 4), z + 4, core)
                up += [(here[x], here[x + 1]) for x in range(3)]
                down += [(here[x + 1], here[x]) for x in range(3)]
                far += [(here[3], after), (here[0], before)]
                relay += [(here[3], here[2]), (here[0], here[1])]
                carry += [(here[2], after), (here[1], before)]
    return up, down, far, relay, carry


def in_hbm(value):
    return pltpu.with_memory_space_constraint(value, pltpu.HBM)


def limit(mib):
    return pltpu.CompilerParams(vmem_limit_bytes=mib << 20)


def step(phase_field, kappa_table, eps_table, orient_index, family_index):
    groups = lax.axis_size("vert")
    runs = groups // 2
    variants = phase_field.shape[0]
    place = lax.axis_index("vert")
    core = (place % 2).astype(jnp.int32)
    slab = lax.axis_index("gx")
    kz_own = (
        place // 2 * 32 + slab // 8 * 1 + slab // 4 % 2 * 16 + slab % 4 * 4
    ).astype(jnp.int32)
    place_arr = jnp.stack([core, kz_own, (lax.axis_index("gx") % SLAB).astype(jnp.int32)])
    eps_t, kappa_t = eps_table.T, kappa_table.T

    tz = z_table()
    ry, rp = y_tables()
    hbm = pl.BlockSpec(memory_space=pltpu.HBM)

    planes = [pltpu.HBM((count, NY, NZ), F32) for count in (variants, variants // 2)]
    spread = jax.ShapeDtypeStruct((1024, 128), F32)
    keep, send, last, front, far, relay = pl.pallas_call(
        sums_kernel,
        in_specs=[smem()] + [hbm] * 4,
        out_specs=[vmem()] * 6,
        out_shape=[spread] * 2 + [planes[0]] * 2 + [planes[1]] * 2,
        scratch_shapes=[
            pltpu.VMEM(phase_field.shape, F32),
            pltpu.VMEM((6, 256, 256), BF16),
            pltpu.VMEM((COMPS * 128, NZ), F32),
            pltpu.VMEM((128, NZ), F32),
            pltpu.SMEM(family_index.shape, jnp.int32),
            pltpu.SMEM(eps_t.shape, F32),
            pltpu.SemaphoreType.DMA((SLAB + 3,)),
        ],
        compiler_params=limit(24),
        cost_estimate=pl.CostEstimate(flops=10**8, bytes_accessed=9 << 20, transcendentals=0),
        name="sums",
    )(place_arr, *(in_hbm(value) for value in (family_index, eps_t, phase_field, stacked_halves(tz, ry, rp))))

    partner = [(i, i ^ 1) for i in range(groups)]
    same_core = [[g * groups + 2 * r + c for g, r in MEMBERS] for c in range(2)]

    def exchange(value):
        return lax.all_to_all(
            value, ("gx", "vert"), split_axis=0, concat_axis=0, axis_index_groups=same_core, tiled=True
        )

    received = lax.ppermute(send, "vert", partner)
    summed = keep + received
    both = ("gx", "vert")
    up, down, across, handed, carried = halo_routes()
    relay = lax.ppermute(relay, both, handed)
    near_low = lax.ppermute(last, both, up)
    near_high = lax.ppermute(front, both, down)
    far = lax.ppermute(far, both, across)
    carry = lax.ppermute(relay, both, carried)

    arrived = exchange(summed.reshape(128, 8, 128)).reshape(1, runs, 32, 8, 128)

    answers = pl.pallas_call(
        spectral_kernel,
        in_specs=[smem()] + [vmem()] * 2,
        out_specs=vmem(),
        out_shape=jax.ShapeDtypeStruct((1, runs, 32, 8, 128), F32),
        compiler_params=limit(12),
        cost_estimate=pl.CostEstimate(flops=10**8, bytes_accessed=4 << 20, transcendentals=0),
        name="spectral",
    )(place_arr, arrived, spectral_tables(*x_tables()))

    mine = exchange(answers.reshape(128, 8, 128)).reshape(1024, 128)
    other = lax.ppermute(mine, "vert", partner)

    edge_low, edge_high = pl.pallas_call(
        edges_kernel,
        in_specs=[smem()] * 3 + [vmem()] * 4,
        out_specs=[vmem()] * 2,
        out_shape=[pltpu.HBM((variants, NY, NZ), F32)] * 2,
        compiler_params=limit(4),
        cost_estimate=pl.CostEstimate(flops=10**6, bytes_accessed=3 << 20, transcendentals=0),
        name="edges",
    )(place_arr, orient_index, kappa_t, near_low, near_high, far, carry)

    orients = [orient_index[: variants // 2], orient_index[variants // 2 :]]
    part = pl.pallas_call(
        local_kernel,
        in_specs=[smem()] * 3 + [vmem()],
        out_specs=vmem(),
        out_shape=pltpu.HBM(phase_field.shape, F32),
        compiler_params=limit(8),
        cost_estimate=pl.CostEstimate(flops=10**7, bytes_accessed=10 << 20, transcendentals=0),
        name="local",
    )(*orients, kappa_t, phase_field)

    per_step = 8
    whole = pl.BlockSpec((per_step, SLAB, NY, NZ), lambda i: (i, 0, 0, 0))
    phase_next, stress = pl.pallas_call(
        update_kernel,
        grid=(variants // per_step,),
        in_specs=[smem()] * 3 + [vmem()] * 4 + [hbm] * 3,
        out_specs=[whole, pl.BlockSpec((COMPS, SLAB, NY, NZ), lambda i: (0, 0, 0, 0))],
        out_shape=[
            jax.ShapeDtypeStruct(phase_field.shape, F32),
            jax.ShapeDtypeStruct((COMPS, SLAB, NY, NZ), F32),
        ],
        scratch_shapes=[
            pltpu.VMEM((SLAB, NY, NZ), F32),
            pltpu.VMEM((variants, NY, NZ), F32),
            pltpu.VMEM((variants, NY, NZ), F32),
            pltpu.VMEM(phase_field.shape, F32),
            pltpu.SemaphoreType.DMA((variants // per_step + 2,)),
        ],
        compiler_params=limit(26),
        cost_estimate=pl.CostEstimate(flops=10**8, bytes_accessed=12 << 20, transcendentals=0),
        name="update",
    )(
        place_arr, family_index, eps_t, mine, other,
        stacked_halves(np.linalg.inv(ry), np.linalg.inv(rp), np.linalg.inv(tz).T),
        phase_field, *(in_hbm(value) for value in (edge_low, edge_high, part)),
    )
    return phase_next, stress


def solution(mesh):
    return jax.shard_map(
        step,
        mesh=mesh,
        in_specs=(P("vert", "gx", None, None), P(), P(), P("vert"), P("vert")),
        out_specs=(P("vert", "gx", None, None), P(None, "gx", None, None)),
        check_vma=False,
    )
```
